32 devices in a mesh: cuts: 16 (over z, x, core), ang: 2 (over y).
Axes of the slice: x: 2, y: 2, z: 4, core: 2. Of those that a mesh axis runs over, the one named last changes fastest.
Arguments:
- projections: bfloat16 [16, 16, 2, 128, 256], P('cuts', None, 'ang'), may hold values from -48 to 48
- start_image: bfloat16 [4096, 1024], P('cuts'), may hold values from 0 to 2
- system: bfloat16 [8, 16, 2, 64, 128], P('ang'), may hold values from 0.0009994507 to 0.029907227
- first_tile: int32 [8, 16], P('ang'), may hold values from 0 to 3, as said below
Outputs:
- new_image: float32 [4096, 1024], P('cuts', 'ang')
- residual: bfloat16 [16, 4096, 256], P('ang', 'cuts')
The draws below stay inside these ranges and needn't reach their ends.
Inputs may be any that keep to these rules, and one draw needn't show every extreme that they name: In every angle block each bin tile is first_tile of at least one pixel tile; every pixel tile meets exactly two bin tiles, first_tile and first_tile + 1 modulo 4.
All inputs are finite; a program needn't handle non-finite values.
Results may differ from the reference program's by a relative error of at most 0.001.
Values may be sent and summed in bfloat16 or wider, within the bound.
A program may use at most 128 MiB of HBM per device.

```python
import jax
import jax.numpy as jnp
from jax import lax

TILE_WIDTH = 64
PAIR_ANG = 2
BIN_TILE_COUNT = 4
PIXEL_TILES = 16
ANGLE_COUNT = 16
BLOCKS = 8
ROWS = 4096
SLICE_BLOCKS = 16
ROW_GROUPS = 2
GROUP_SLICES = 128
NPIX = 1024
DETECTOR_BINS = 256


def draw_first_tile(key, part):
    base_key = jax.random.fold_in(key, 31)
    order_key = jax.random.fold_in(key, 47)
    base = jax.random.randint(base_key, (BLOCKS, PIXEL_TILES), 0, BIN_TILE_COUNT, dtype=jnp.int32)

    def one_order(subkey):
        return jax.random.permutation(subkey, PIXEL_TILES)
    orders = jax.vmap(one_order)(jax.random.split(order_key, BLOCKS))
    ranks = jnp.argsort(orders, axis=1, stable=True).astype(jnp.int32)
    return jnp.where(ranks < BIN_TILE_COUNT, ranks, base).astype(jnp.int32)


def levels(rng, shape, cuts, least, high):
    def one(dim, shards_of):
        draws = jax.random.uniform(jax.random.fold_in(jax.random.fold_in(rng, 6), dim), (shards_of,), jnp.float32, least / len(cuts), high / len(cuts))
        return jnp.repeat(jnp.exp(draws), shape[dim] // shards_of).reshape((-1,) + (1,) * (len(shape) - dim - 1))

    factor_of = one(*cuts[0])
    for cut in cuts[1:]:
        factor_of = factor_of * one(*cut)
    return factor_of


def scatter_about(stream_key, shape, spread, bound, cuts=(), kind=jnp.bfloat16):
    level = levels(stream_key, shape, cuts, -0.22, 0.18) if cuts else 1.0
    result = jax.random.normal(stream_key, shape, jnp.float32) * spread * level
    return jnp.minimum(jnp.maximum(result, -bound), bound).astype(kind)


def setup_inputs(seed: int = 0) -> dict:
    key_of = jax.random.split(jax.random.key(seed), 5)
    return {
        "projections": scatter_about(key_of[0], (ANGLE_COUNT, SLICE_BLOCKS, ROW_GROUPS, GROUP_SLICES, DETECTOR_BINS), (0.031 * TILE_WIDTH * PIXEL_TILES / BIN_TILE_COUNT), 48.0, ((0, 16), (2, 2))),
        "start_image": jnp.clip(2.0 * jax.random.uniform(key_of[1], (ROWS, NPIX), jnp.float32) ** levels(key_of[1], (ROWS, NPIX), ((0, 16),), -0.2, 0.2), 0.0, 2.0).astype(jnp.bfloat16),
        "system": jnp.clip(0.0009994507 + 0.028907776 * jax.random.uniform(key_of[2], (BLOCKS, PIXEL_TILES, 2, TILE_WIDTH, PAIR_ANG * TILE_WIDTH), jnp.float32) ** levels(key_of[2], (BLOCKS, PIXEL_TILES, 2, TILE_WIDTH, PAIR_ANG * TILE_WIDTH), ((0, 2),), -0.2, 0.2), 0.0009994507, 0.029907227).astype(jnp.bfloat16),
        "first_tile": draw_first_tile(jax.random.fold_in(key_of[4], 71), 0),
    }


def reference(projections, start_image, system, first_tile):
    sinogram = projections.reshape(BLOCKS, PAIR_ANG, ROWS, DETECTOR_BINS)
    pixels = start_image.astype(jnp.float32).reshape(ROWS, PIXEL_TILES, TILE_WIDTH)
    tile_ids = jnp.arange(BIN_TILE_COUNT, dtype=jnp.int32)
    highest = lax.Precision.HIGHEST

    def step_block(carry, inputs):
        backproj, col_total = carry
        weights, first, measured = inputs
        weights = weights.astype(jnp.float32)
        bin_index = jnp.stack([first, (first + 1) % BIN_TILE_COUNT], axis=1)
        onehot = (bin_index[:, :, None] == tile_ids).astype(jnp.float32)
        partial_value = jnp.einsum('rpi,pjic->pjrc', pixels, weights, precision=highest)
        forward = jnp.einsum('pjb,pjrc->brc', onehot, partial_value, precision=highest)
        row_total = jnp.einsum('pjb,pjc->bc', onehot, jnp.sum(weights, axis=2), precision=highest)
        measured_t = measured.astype(jnp.float32).reshape(PAIR_ANG, ROWS, BIN_TILE_COUNT, TILE_WIDTH)
        measured_t = measured_t.transpose(2, 1, 0, 3).reshape(BIN_TILE_COUNT, ROWS, PAIR_ANG * TILE_WIDTH)
        resid = ((measured_t - forward) / row_total[:, None, :]).astype(jnp.bfloat16)
        resid = lax.optimization_barrier(resid)
        picked = jnp.einsum('pjb,brc->pjrc', onehot, resid.astype(jnp.float32), precision=highest)
        backproj = backproj + jnp.einsum('pjrc,pjic->rpi', picked, weights, precision=highest)
        col_total = col_total + jnp.sum(weights, axis=(1, 3))
        out_block = resid.reshape(BIN_TILE_COUNT, ROWS, PAIR_ANG, TILE_WIDTH).transpose(2, 1, 0, 3).reshape(PAIR_ANG, ROWS, DETECTOR_BINS)
        return (backproj, col_total), out_block

    start = (jnp.zeros((ROWS, PIXEL_TILES, TILE_WIDTH), jnp.float32), jnp.zeros((PIXEL_TILES, TILE_WIDTH), jnp.float32))
    (backproj, col_total), blocks_out = lax.scan(step_block, start, (system, first_tile, sinogram))
    residual = blocks_out.reshape(ANGLE_COUNT, ROWS, DETECTOR_BINS)
    new_image = start_image.astype(jnp.float32) + (backproj / col_total[None, :, :]).reshape(ROWS, NPIX)
    return new_image, residual
```

```python
import functools

import jax
import jax.numpy as jnp
from jax import lax
from jax.experimental import pallas as pl
from jax.experimental.pallas import tpu as pltpu
from jax.sharding import PartitionSpec as P

MESH = pl.DeviceIdType.MESH
NT = (((1,), (1,)), ((), ()))
SPLIT = (3, 2, 1, 1, 1)
TURN = (0, 1, 2, 2, 2)
LATE = 3
PUTS = 2
PAD = 16
VMEM_BYTES = 67043328


def kernel(
    C, G, sizes, first_in, proj, image, system, new_out, res_out,
    first, img, sysv, A, F, R, arr, U, own, urecv, colp, crecv,
    first_sem, img_sem, sys_sem, send_sem, arr_sem, go_sem,
    usend_sem, urecv_sem, csend_sem, crecv_sem,
):
    c = lax.axis_index("cuts")
    a = lax.axis_index("ang")
    T = C // G
    blocks, ptiles, _, W, PW = system.shape
    KR = proj.shape[3]
    NC = len(sizes)
    starts = [sum(sizes[:q]) for q in range(NC)]
    slices, npix = image.shape
    share = npix // G
    bins = proj.shape[4]
    ntiles = bins // W
    pair = PW // W

    tgt = c // T
    slot = a * T + lax.rem(c, T)

    barrier = pltpu.get_barrier_semaphore()
    for i in range(T):
        source = a * T + lax.rem(c + i, T)
        for s in range(1 if i == 0 else 0, G):
            pl.semaphore_signal(
                barrier, inc=1, device_id=(source, lax.rem(a + s, G)), device_id_type=MESH
            )

    @pl.when(tgt != a)
    def _():
        pl.semaphore_signal(
            barrier, inc=1, device_id=(a * T + lax.rem(c, T), a), device_id_type=MESH
        )

    for s in range(1, G):
        pl.semaphore_signal(barrier, inc=1, device_id=(c, lax.rem(a + s, G)), device_id_type=MESH)

    def flip(m):
        o = c
        for b in range(C.bit_length() - 1):
            if (m >> b) & 1:
                o = o + (1 - 2 * lax.rem(c // (1 << b), 2)) * (1 << b)
        return o

    paced = G == 2 and C & (C - 1) == 0 and T > 1
    mate = flip(T // 2) if paced else c
    if paced:
        @pl.when(tgt != a)
        def _():
            pl.semaphore_signal(barrier, inc=1, device_id=(mate, a), device_id_type=MESH)

    sys_copy = pltpu.make_async_copy(system, sysv, sys_sem)
    sys_copy.start()
    first_copy = pltpu.make_async_copy(first_in, first, first_sem)
    first_copy.start()
    img_copies = []
    for q in range(NC):
        for b in range(G):
            cp = pltpu.make_async_copy(
                image.at[pl.ds(b * KR + starts[q], sizes[q])],
                img.at[pl.ds(G * starts[q] + b * sizes[q], sizes[q])],
                img_sem.at[q, b],
            )
            cp.start()
            img_copies.append(cp)
    away = jnp.where(tgt == a, 0, 1)
    pl.semaphore_wait(barrier, C + G - 2 + (2 * away if paced else away))

    def piece(q, o):
        return pltpu.make_async_remote_copy(
            src_ref=proj.at[0, o, 0, pl.ds(starts[q], sizes[q])],
            dst_ref=arr[q].at[slot],
            send_sem=send_sem.at[q],
            recv_sem=arr_sem.at[q],
            device_id=(o, tgt),
            device_id_type=MESH,
        )

    turn = TURN[:NC] if paced and NC == len(TURN) else (0,) * NC
    turns = max(turn) + 1
    inner = tgt + lax.rem(c, T) // max(T // 2, 1) == 1
    order = [flip(m) for m in range(C - 1, 0, -1)] if paced else [lax.rem(c + s, C) for s in range(1, C)]
    AHEAD = 2 if paced else 0

    def send_ahead(q):
        if AHEAD and q < NC:
            @pl.when(tgt == G - 1)
            def _():
                for o in range(AHEAD):
                    piece(q, o).start()

    def send_rest(q):
        for o in order:
            if AHEAD:
                @pl.when((tgt != G - 1) | (o >= AHEAD))
                def _(o=o):
                    piece(q, o).start()
            else:
                piece(q, o).start()

        @pl.when(tgt != a)
        def _():
            piece(q, c).start()

        @pl.when(tgt == a)
        def _():
            pltpu.make_async_copy(
                proj.at[0, c, 0, pl.ds(starts[q], sizes[q])], arr[q].at[slot], arr_sem.at[q]
            ).start()

    def send(q):
        send_ahead(q + 1)
        send_rest(q)

    def sent(q):
        rows = pl.ds(starts[q], sizes[q])

        @pl.when(tgt == a)
        def _():
            part = proj.at[0, pl.ds(0, C - 1), 0, rows]
            pltpu.make_async_copy(part, part, send_sem.at[q]).wait()

        @pl.when(tgt != a)
        def _():
            part = proj.at[0, :, 0, rows]
            pltpu.make_async_copy(part, part, send_sem.at[q]).wait()

    def of_turn(k):
        return [q for q in range(NC) if turn[q] == k]

    send_ahead(0)
    for q in of_turn(0):
        send(q)
    if turns > 1:
        @pl.when(inner)
        def _():
            for k in range(1, turns):
                for q in of_turn(k):
                    send(q)

    def take_turn(k):
        if k >= turns:
            return

        @pl.when(inner)
        def _():
            for q in of_turn(k - 1):
                sent(q)
            pl.semaphore_signal(go_sem.at[k - 1], inc=1, device_id=(mate, a), device_id_type=MESH)

        @pl.when(jnp.logical_not(inner))
        def _():
            pl.semaphore_wait(go_sem.at[k - 1], 1)
            for q in of_turn(k):
                send(q)

    img[pl.ds(slices, PAD)] = jnp.ones((PAD, npix), jnp.bfloat16)
    R[pl.ds(0, PAD)] = jnp.ones((PAD, T * bins), jnp.bfloat16)
    sys_copy.wait()
    first_copy.wait()

    def build(i, carry):
        lane = lax.broadcasted_iota(jnp.int32, (W, pair * W), 1) // W
        cols = pl.ds(pl.multiple_of(i * pair * W, pair * W), pair * W)
        for g in range(blocks):
            x = [
                jnp.concatenate([sysv[g, i * pair + k, j] for k in range(pair)], axis=0)
                .astype(jnp.float32).T.astype(jnp.bfloat16)
                for j in range(2)
            ]
            f = jnp.full(lane.shape, first[g, i * pair], jnp.int32)
            for k in range(1, pair):
                f = jnp.where(lane == k, first[g, i * pair + k], f)
            second = jnp.where(f == ntiles - 1, 0, f + 1)
            for b in range(ntiles):
                m0, m1 = f == b, second == b
                for t in range(pair):
                    part = slice(t * W, (t + 1) * W)
                    tile = jnp.where(m0, x[0][part], jnp.where(m1, x[1][part], jnp.zeros((), jnp.bfloat16)))
                    A[pl.ds((g * pair + t) * bins + b * W, W), cols] = tile
        return carry

    lax.fori_loop(0, ptiles // pair, build, 0)

    for cp in img_copies:
        cp.wait()

    def project(t, carry):
        m = A[pl.ds(pl.multiple_of(t * bins, bins), bins)]
        F[t] = lax.dot_general(img[...], m, NT, preferred_element_type=jnp.float32)
        return carry

    lax.fori_loop(0, T, project, 0)

    def residual_part(q):
        def body(t, carry):
            scale = 1.0 / F[t, pl.ds(slices, 8)][:1]
            for b in range(G):
                value = arr[q][b * T + t].astype(jnp.float32)
                f = F[t, pl.ds(G * starts[q] + b * sizes[q], sizes[q])]
                res = ((value - f) * scale).astype(jnp.bfloat16)
                R[
                    pl.ds(PAD + G * starts[q] + b * sizes[q], sizes[q]),
                    pl.ds(pl.multiple_of(t * bins, bins), bins),
                ] = res
                res_out[t, pl.ds(b * KR + starts[q], sizes[q])] = res
            return carry

        lax.fori_loop(0, T, body, 0)

    def back(lo, hi, g):
        return jnp.dot(
            R[pl.ds(lo, hi - lo)],
            A[:, pl.ds(pl.multiple_of(g * share, share), share)],
            preferred_element_type=jnp.float32,
        )

    def col_copy(s):
        g = lax.rem(a + s, G)
        return pltpu.make_async_remote_copy(
            src_ref=colp.at[g], dst_ref=crecv.at[s - 1], send_sem=csend_sem.at[s - 1],
            recv_sem=crecv_sem, device_id=(c, g), device_id_type=MESH,
        )

    def u_copy(q, s):
        g = lax.rem(a + s, G)
        return pltpu.make_async_remote_copy(
            src_ref=U[q].at[s - 1], dst_ref=urecv[q].at[s - 1],
            send_sem=usend_sem.at[q, s - 1], recv_sem=urecv_sem.at[q, s - 1],
            device_id=(c, g), device_id_type=MESH,
        )

    def own_back(lo, hi):
        y = back(lo, hi, a)
        if lo == 0:
            colp[a] = y[:8]
            y = y[PAD:]
            lo = PAD
        own[pl.ds(lo - PAD, hi - lo)] = y

    def process(q):
        pltpu.make_async_copy(arr[q], arr[q], arr_sem.at[q]).wait()
        residual_part(q)
        lo = 0 if q == 0 else PAD + G * starts[q]
        hi = PAD + G * (starts[q] + sizes[q])
        for s in range(1, G):
            y = back(lo, hi, lax.rem(a + s, G))
            if q == 0:
                colp[lax.rem(a + s, G)] = y[:8]
                y = y[PAD:]
            U[q][s - 1] = y
            u_copy(q, s).start()
            if q == 0:
                col_copy(s).start()
        late = max(NC - LATE, 0)
        if q < late:
            own_back(lo, hi)
        elif q == NC - 1:
            own_back(0 if late == 0 else PAD + G * starts[late], hi)

    def finish(q, own_inv):
        total = own[pl.ds(G * starts[q], G * sizes[q])]
        for s in range(1, G):
            u_copy(q, s).wait_recv()
            total = total + urecv[q][s - 1]
        mine = img[
            pl.ds(G * starts[q], G * sizes[q]), pl.ds(pl.multiple_of(a * share, share), share)
        ]
        new = mine.astype(jnp.float32) + total * own_inv
        for b in range(G):
            new_out[pl.ds(b * KR + starts[q], sizes[q])] = new[b * sizes[q] : (b + 1) * sizes[q]]

    take_turn(1)
    for q in range(NC):
        process(q)
        take_turn(q + 2)

    pltpu.make_async_copy(crecv, crecv, crecv_sem).wait()
    columns = colp[a][:1]
    for s in range(1, G):
        columns = columns + crecv[s - 1][:1]
    own_inv = 1.0 / columns
    for q in range(NC):
        finish(q, own_inv)

    for q in range(NC):
        if turn[q] == turns - 1:
            sent(q)
        else:
            @pl.when(jnp.logical_not(inner))
            def _(q=q):
                sent(q)

    for s in range(1, G):
        col_copy(s).wait_send()
    for q in range(NC):
        for s in range(1, G):
            u_copy(q, s).wait_send()


def put_out(new_in, res_in, new_out, res_out, sem):
    copies = []
    for i, (src, dst) in enumerate(((new_in, new_out), (res_in, res_out))):
        n = src.shape[0] // PUTS
        for k in range(PUTS):
            part = pl.ds(k * n, n)
            copies.append(pltpu.make_async_copy(src.at[part], dst.at[part], sem.at[i * PUTS + k]))
    for cp in copies:
        cp.start()
    for cp in copies:
        cp.wait()


def chunk_sizes(rows):
    unit = max(16, rows // sum(SPLIT))
    sizes = [n * unit for n in SPLIT]
    if sum(sizes) == rows:
        return sizes
    return [16] * (rows // 16) if rows % 16 == 0 else [rows]


def on_device(C, G, projections, start_image, system, first_tile):
    T = C // G
    KR = projections.shape[3]
    sizes = chunk_sizes(KR)
    NC = len(sizes)
    slices, npix = start_image.shape
    bins = projections.shape[4]
    share = npix // G
    bf16, f32 = jnp.bfloat16, jnp.float32
    dma = pltpu.SemaphoreType.DMA
    out_bytes = slices * share * 4 + T * slices * bins * 2
    new_image, residual = pl.pallas_call(
        functools.partial(kernel, C, G, sizes),
        out_shape=(
            pltpu.VMEM((slices, share), f32),
            pltpu.VMEM((T, slices, bins), bf16),
        ),
        in_specs=[pl.BlockSpec(memory_space=pltpu.HBM)] * 4,
        out_specs=(pl.BlockSpec(memory_space=pltpu.VMEM),) * 2,
        scratch_shapes=[
            pltpu.SMEM(first_tile.shape, jnp.int32),
            pltpu.VMEM((slices + PAD, npix), bf16),
            pltpu.VMEM(system.shape, bf16),
            pltpu.VMEM((T * bins, npix), bf16),
            pltpu.VMEM((T, slices + PAD, bins), f32),
            pltpu.VMEM((slices + PAD, T * bins), bf16),
            [pltpu.VMEM((C, n, bins), bf16) for n in sizes],
            [pltpu.VMEM((G - 1, G * n, share), f32) for n in sizes],
            pltpu.VMEM((slices, share), f32),
            [pltpu.VMEM((G - 1, G * n, share), f32) for n in sizes],
            pltpu.VMEM((G, 8, share), f32),
            pltpu.VMEM((G - 1, 8, share), f32),
            dma,
            dma((NC, G)),
            dma,
            dma((NC,)),
            dma((NC,)),
            pltpu.SemaphoreType.REGULAR((max(NC, 2),)),
            dma((NC, G - 1)),
            dma((NC, G - 1)),
            dma((G - 1,)),
            dma,
        ],
        compiler_params=pltpu.CompilerParams(
            collective_id=0, has_side_effects=True, vmem_limit_bytes=VMEM_BYTES - out_bytes
        ),
    )(first_tile, projections, start_image, system)
    return pl.pallas_call(
        put_out,
        out_shape=(
            jax.ShapeDtypeStruct(new_image.shape, f32),
            jax.ShapeDtypeStruct(residual.shape, bf16),
        ),
        in_specs=[pl.BlockSpec(memory_space=pl.ANY)] * 2,
        out_specs=(pl.BlockSpec(memory_space=pl.ANY),) * 2,
        scratch_shapes=[dma((2 * PUTS,))],
        compiler_params=pltpu.CompilerParams(vmem_limit_bytes=1 << 20),
    )(new_image, residual)


def solution(mesh):
    in_specs = (
        P("cuts", None, "ang", None, None),
        P("cuts", None),
        P("ang", None, None, None, None),
        P("ang", None),
    )
    out_specs = (P("cuts", "ang"), P("ang", "cuts", None))
    return jax.shard_map(
        functools.partial(on_device, mesh.shape["cuts"], mesh.shape["ang"]),
        mesh=mesh, in_specs=in_specs, out_specs=out_specs, check_vma=False,
    )
```

```python
import functools

import jax
import jax.numpy as jnp
from jax import lax
from jax.experimental import pallas as pl
from jax.experimental.pallas import tpu as pltpu
from jax.sharding import PartitionSpec as P

MESH = pl.DeviceIdType.MESH
NT = (((1,), (1,)), ((), ()))
SPLIT = (3, 2, 1, 1, 1)
TURN = (0, 1, 2, 2, 2)
LATE = 3
PUTS = 2
PAD = 16
STEPS = 32767.0
TINY = 1e-30
VMEM_BYTES = 67043328


def kernel(
    C, G, sizes, first_in, proj, image, system, new_out, res_out,
    first, img, sysv, A, F, R, arr, U, unit, own, urecv, unitrecv, colp, crecv,
    first_sem, img_sem, sys_sem, send_sem, arr_sem, go_sem,
    usend_sem, urecv_sem, nsend_sem, nrecv_sem, csend_sem, crecv_sem,
):
    c = lax.axis_index("cuts")
    a = lax.axis_index("ang")
    T = C // G
    blocks, ptiles, _, W, PW = system.shape
    KR = proj.shape[3]
    NC = len(sizes)
    starts = [sum(sizes[:q]) for q in range(NC)]
    slices, npix = image.shape
    share = npix // G
    bins = proj.shape[4]
    ntiles = bins // W
    pair = PW // W

    tgt = c // T
    slot = a * T + lax.rem(c, T)

    barrier = pltpu.get_barrier_semaphore()
    for i in range(T):
        source = a * T + lax.rem(c + i, T)
        for s in range(1 if i == 0 else 0, G):
            pl.semaphore_signal(
                barrier, inc=1, device_id=(source, lax.rem(a + s, G)), device_id_type=MESH
            )

    @pl.when(tgt != a)
    def _():
        pl.semaphore_signal(
            barrier, inc=1, device_id=(a * T + lax.rem(c, T), a), device_id_type=MESH
        )

    for s in range(1, G):
        pl.semaphore_signal(barrier, inc=1, device_id=(c, lax.rem(a + s, G)), device_id_type=MESH)

    def flip(m):
        o = c
        for b in range(C.bit_length() - 1):
            if (m >> b) & 1:
                o = o + (1 - 2 * lax.rem(c // (1 << b), 2)) * (1 << b)
        return o

    paced = G == 2 and C & (C - 1) == 0 and T > 1
    mate = flip(T // 2) if paced else c
    if paced:
        @pl.when(tgt != a)
        def _():
            pl.semaphore_signal(barrier, inc=1, device_id=(mate, a), device_id_type=MESH)

    sys_copy = pltpu.make_async_copy(system, sysv, sys_sem)
    sys_copy.start()
    first_copy = pltpu.make_async_copy(first_in, first, first_sem)
    first_copy.start()
    img_copies = []
    for q in range(NC):
        for b in range(G):
            cp = pltpu.make_async_copy(
                image.at[pl.ds(b * KR + starts[q], sizes[q])],
                img.at[pl.ds(G * starts[q] + b * sizes[q], sizes[q])],
                img_sem.at[q, b],
            )
            cp.start()
            img_copies.append(cp)
    away = jnp.where(tgt == a, 0, 1)
    pl.semaphore_wait(barrier, C + G - 2 + (2 * away if paced else away))

    def piece(q, o):
        return pltpu.make_async_remote_copy(
            src_ref=proj.at[0, o, 0, pl.ds(starts[q], sizes[q])],
            dst_ref=arr[q].at[slot],
            send_sem=send_sem.at[q],
            recv_sem=arr_sem.at[q],
            device_id=(o, tgt),
            device_id_type=MESH,
        )

    turn = TURN[:NC] if paced and NC == len(TURN) else (0,) * NC
    turns = max(turn) + 1
    inner = tgt + lax.rem(c, T) // max(T // 2, 1) == 1
    order = [flip(m) for m in range(C - 1, 0, -1)] if paced else [lax.rem(c + s, C) for s in range(1, C)]
    AHEAD = 2 if paced else 0

    def send_ahead(q):
        if AHEAD and q < NC:
            @pl.when(tgt == G - 1)
            def _():
                for o in range(AHEAD):
                    piece(q, o).start()

    def send_rest(q):
        for o in order:
            if AHEAD:
                @pl.when((tgt != G - 1) | (o >= AHEAD))
                def _(o=o):
                    piece(q, o).start()
            else:
                piece(q, o).start()

        @pl.when(tgt != a)
        def _():
            piece(q, c).start()

        @pl.when(tgt == a)
        def _():
            pltpu.make_async_copy(
                proj.at[0, c, 0, pl.ds(starts[q], sizes[q])], arr[q].at[slot], arr_sem.at[q]
            ).start()

    def send(q):
        send_ahead(q + 1)
        send_rest(q)

    def sent(q):
        rows = pl.ds(starts[q], sizes[q])

        @pl.when(tgt == a)
        def _():
            part = proj.at[0, pl.ds(0, C - 1), 0, rows]
            pltpu.make_async_copy(part, part, send_sem.at[q]).wait()

        @pl.when(tgt != a)
        def _():
            part = proj.at[0, :, 0, rows]
            pltpu.make_async_copy(part, part, send_sem.at[q]).wait()

    def of_turn(k):
        return [q for q in range(NC) if turn[q] == k]

    send_ahead(0)
    for q in of_turn(0):
        send(q)
    if turns > 1:
        @pl.when(inner)
        def _():
            for k in range(1, turns):
                for q in of_turn(k):
                    send(q)

    def take_turn(k):
        if k >= turns:
            return

        @pl.when(inner)
        def _():
            for q in of_turn(k - 1):
                sent(q)
            pl.semaphore_signal(go_sem.at[k - 1], inc=1, device_id=(mate, a), device_id_type=MESH)

        @pl.when(jnp.logical_not(inner))
        def _():
            pl.semaphore_wait(go_sem.at[k - 1], 1)
            for q in of_turn(k):
                send(q)

    img[pl.ds(slices, PAD)] = jnp.ones((PAD, npix), jnp.bfloat16)
    R[pl.ds(0, PAD)] = jnp.ones((PAD, T * bins), jnp.bfloat16)
    sys_copy.wait()
    first_copy.wait()

    def build(i, carry):
        lane = lax.broadcasted_iota(jnp.int32, (W, pair * W), 1) // W
        cols = pl.ds(pl.multiple_of(i * pair * W, pair * W), pair * W)
        for g in range(blocks):
            x = [
                jnp.concatenate([sysv[g, i * pair + k, j] for k in range(pair)], axis=0)
                .astype(jnp.float32).T.astype(jnp.bfloat16)
                for j in range(2)
            ]
            f = jnp.full(lane.shape, first[g, i * pair], jnp.int32)
            for k in range(1, pair):
                f = jnp.where(lane == k, first[g, i * pair + k], f)
            second = jnp.where(f == ntiles - 1, 0, f + 1)
            for b in range(ntiles):
                m0, m1 = f == b, second == b
                for t in range(pair):
                    part = slice(t * W, (t + 1) * W)
                    tile = jnp.where(m0, x[0][part], jnp.where(m1, x[1][part], jnp.zeros((), jnp.bfloat16)))
                    A[pl.ds((g * pair + t) * bins + b * W, W), cols] = tile
        return carry

    lax.fori_loop(0, ptiles // pair, build, 0)

    for cp in img_copies:
        cp.wait()

    def project(t, carry):
        m = A[pl.ds(pl.multiple_of(t * bins, bins), bins)]
        F[t] = lax.dot_general(img[...], m, NT, preferred_element_type=jnp.float32)
        return carry

    lax.fori_loop(0, T, project, 0)

    def residual_part(q):
        def body(t, carry):
            scale = 1.0 / F[t, pl.ds(slices, 8)][:1]
            for b in range(G):
                value = arr[q][b * T + t].astype(jnp.float32)
                f = F[t, pl.ds(G * starts[q] + b * sizes[q], sizes[q])]
                res = ((value - f) * scale).astype(jnp.bfloat16)
                R[
                    pl.ds(PAD + G * starts[q] + b * sizes[q], sizes[q]),
                    pl.ds(pl.multiple_of(t * bins, bins), bins),
                ] = res
                res_out[t, pl.ds(b * KR + starts[q], sizes[q])] = res
            return carry

        lax.fori_loop(0, T, body, 0)

    def back(lo, hi, g):
        return jnp.dot(
            R[pl.ds(lo, hi - lo)],
            A[:, pl.ds(pl.multiple_of(g * share, share), share)],
            preferred_element_type=jnp.float32,
        )

    def col_copy(s):
        g = lax.rem(a + s, G)
        return pltpu.make_async_remote_copy(
            src_ref=colp.at[g], dst_ref=crecv.at[s - 1], send_sem=csend_sem.at[s - 1],
            recv_sem=crecv_sem, device_id=(c, g), device_id_type=MESH,
        )

    def u_copy(q, s):
        g = lax.rem(a + s, G)
        return pltpu.make_async_remote_copy(
            src_ref=U[q].at[s - 1], dst_ref=urecv[q].at[s - 1],
            send_sem=usend_sem.at[q, s - 1], recv_sem=urecv_sem.at[q, s - 1],
            device_id=(c, g), device_id_type=MESH,
        )

    def unit_copy(q, s):
        g = lax.rem(a + s, G)
        return pltpu.make_async_remote_copy(
            src_ref=unit[q].at[s - 1], dst_ref=unitrecv[q].at[s - 1],
            send_sem=nsend_sem.at[q, s - 1], recv_sem=nrecv_sem.at[q, s - 1],
            device_id=(c, g), device_id_type=MESH,
        )

    def own_back(lo, hi):
        y = back(lo, hi, a)
        if lo == 0:
            colp[a] = y[:8]
            y = y[PAD:]
            lo = PAD
        own[pl.ds(lo - PAD, hi - lo)] = y

    def process(q):
        pltpu.make_async_copy(arr[q], arr[q], arr_sem.at[q]).wait()
        residual_part(q)
        lo = 0 if q == 0 else PAD + G * starts[q]
        hi = PAD + G * (starts[q] + sizes[q])
        for s in range(1, G):
            y = back(lo, hi, lax.rem(a + s, G))
            if q == 0:
                colp[lax.rem(a + s, G)] = y[:8]
                y = y[PAD:]
            top = jnp.maximum(jnp.max(jnp.abs(y), axis=0, keepdims=True), TINY)
            unit[q][s - 1] = top * (1.0 / STEPS)
            U[q][s - 1] = jnp.round(y * (STEPS / top)).astype(jnp.int32).astype(jnp.int16)
            unit_copy(q, s).start()
            u_copy(q, s).start()
            if q == 0:
                col_copy(s).start()
        late = max(NC - LATE, 0)
        if q < late:
            own_back(lo, hi)
        elif q == NC - 1:
            own_back(0 if late == 0 else PAD + G * starts[late], hi)

    def finish(q, own_inv):
        total = own[pl.ds(G * starts[q], G * sizes[q])]
        for s in range(1, G):
            u_copy(q, s).wait_recv()
            unit_copy(q, s).wait_recv()
            total = total + urecv[q][s - 1].astype(jnp.int32).astype(jnp.float32) * unitrecv[q][s - 1]
        mine = img[
            pl.ds(G * starts[q], G * sizes[q]), pl.ds(pl.multiple_of(a * share, share), share)
        ]
        new = mine.astype(jnp.float32) + total * own_inv
        for b in range(G):
            new_out[pl.ds(b * KR + starts[q], sizes[q])] = new[b * sizes[q] : (b + 1) * sizes[q]]

    take_turn(1)
    for q in range(NC):
        process(q)
        take_turn(q + 2)

    pltpu.make_async_copy(crecv, crecv, crecv_sem).wait()
    columns = colp[a][:1]
    for s in range(1, G):
        columns = columns + crecv[s - 1][:1]
    own_inv = 1.0 / columns
    for q in range(NC):
        finish(q, own_inv)

    for q in range(NC):
        if turn[q] == turns - 1:
            sent(q)
        else:
            @pl.when(jnp.logical_not(inner))
            def _(q=q):
                sent(q)

    for s in range(1, G):
        col_copy(s).wait_send()
    for q in range(NC):
        for s in range(1, G):
            u_copy(q, s).wait_send()
            unit_copy(q, s).wait_send()


def put_out(new_in, res_in, new_out, res_out, sem):
    copies = []
    for i, (src, dst) in enumerate(((new_in, new_out), (res_in, res_out))):
        n = src.shape[0] // PUTS
        for k in range(PUTS):
            part = pl.ds(k * n, n)
            copies.append(pltpu.make_async_copy(src.at[part], dst.at[part], sem.at[i * PUTS + k]))
    for cp in copies:
        cp.start()
    for cp in copies:
        cp.wait()


def chunk_sizes(rows):
    unit = max(16, rows // sum(SPLIT))
    sizes = [n * unit for n in SPLIT]
    if sum(sizes) == rows:
        return sizes
    return [16] * (rows // 16) if rows % 16 == 0 else [rows]


def on_device(C, G, projections, start_image, system, first_tile):
    T = C // G
    KR = projections.shape[3]
    sizes = chunk_sizes(KR)
    NC = len(sizes)
    slices, npix = start_image.shape
    bins = projections.shape[4]
    share = npix // G
    bf16, f32 = jnp.bfloat16, jnp.float32
    dma = pltpu.SemaphoreType.DMA
    out_bytes = slices * share * 4 + T * slices * bins * 2
    new_image, residual = pl.pallas_call(
        functools.partial(kernel, C, G, sizes),
        out_shape=(
            pltpu.VMEM((slices, share), f32),
            pltpu.VMEM((T, slices, bins), bf16),
        ),
        in_specs=[pl.BlockSpec(memory_space=pltpu.HBM)] * 4,
        out_specs=(pl.BlockSpec(memory_space=pltpu.VMEM),) * 2,
        scratch_shapes=[
            pltpu.SMEM(first_tile.shape, jnp.int32),
            pltpu.VMEM((slices + PAD, npix), bf16),
            pltpu.VMEM(system.shape, bf16),
            pltpu.VMEM((T * bins, npix), bf16),
            pltpu.VMEM((T, slices + PAD, bins), f32),
            pltpu.VMEM((slices + PAD, T * bins), bf16),
            [pltpu.VMEM((C, n, bins), bf16) for n in sizes],
            [pltpu.VMEM((G - 1, G * n, share), jnp.int16) for n in sizes],
            [pltpu.VMEM((G - 1, 1, share), f32) for n in sizes],
            pltpu.VMEM((slices, share), f32),
            [pltpu.VMEM((G - 1, G * n, share), jnp.int16) for n in sizes],
            [pltpu.VMEM((G - 1, 1, share), f32) for n in sizes],
            pltpu.VMEM((G, 8, share), f32),
            pltpu.VMEM((G - 1, 8, share), f32),
            dma,
            dma((NC, G)),
            dma,
            dma((NC,)),
            dma((NC,)),
            pltpu.SemaphoreType.REGULAR((max(NC, 2),)),
            dma((NC, G - 1)),
            dma((NC, G - 1)),
            dma((NC, G - 1)),
            dma((NC, G - 1)),
            dma((G - 1,)),
            dma,
        ],
        compiler_params=pltpu.CompilerParams(
            collective_id=0, has_side_effects=True, vmem_limit_bytes=VMEM_BYTES - out_bytes
        ),
    )(first_tile, projections, start_image, system)
    return pl.pallas_call(
        put_out,
        out_shape=(
            jax.ShapeDtypeStruct(new_image.shape, f32),
            jax.ShapeDtypeStruct(residual.shape, bf16),
        ),
        in_specs=[pl.BlockSpec(memory_space=pl.ANY)] * 2,
        out_specs=(pl.BlockSpec(memory_space=pl.ANY),) * 2,
        scratch_shapes=[dma((2 * PUTS,))],
        compiler_params=pltpu.CompilerParams(vmem_limit_bytes=1 << 20),
    )(new_image, residual)


def solution(mesh):
    in_specs = (
        P("cuts", None, "ang", None, None),
        P("cuts", None),
        P("ang", None, None, None, None),
        P("ang", None),
    )
    out_specs = (P("cuts", "ang"), P("ang", "cuts", None))
    return jax.shard_map(
        functools.partial(on_device, mesh.shape["cuts"], mesh.shape["ang"]),
        mesh=mesh, in_specs=in_specs, out_specs=out_specs, check_vma=False,
    )
```

```python
import functools

import jax
import jax.numpy as jnp
from jax import lax
from jax.experimental import pallas as pl
from jax.experimental.pallas import tpu as pltpu
from jax.sharding import PartitionSpec as P

MESH = pl.DeviceIdType.MESH
NT = (((1,), (1,)), ((), ()))
SPLIT = (3, 2, 1, 1, 1)
TURN = (0, 1, 2, 2, 2)
LATE = 3
PUTS = 2
PAD = 16
STEPS = 32767.0
TINY = 1e-30
VMEM_BYTES = 67043328


def kernel(
    C, G, sizes, first_in, proj, image, system, new_out, res_out,
    first, img, sysv, A, F, R, arr, U, unit, own, urecv, unitrecv, colp, crecv,
    first_sem, img_sem, sys_sem, send_sem, arr_sem, go_sem, up_sem,
    usend_sem, urecv_sem, nsend_sem, nrecv_sem, csend_sem, crecv_sem,
):
    c = lax.axis_index("cuts")
    a = lax.axis_index("ang")
    T = C // G
    blocks, ptiles, _, W, PW = system.shape
    KR = proj.shape[3]
    NC = len(sizes)
    starts = [sum(sizes[:q]) for q in range(NC)]
    slices, npix = image.shape
    share = npix // G
    bins = proj.shape[4]
    ntiles = bins // W
    pair = PW // W

    tgt = c // T
    slot = a * T + lax.rem(c, T)

    def flip(m):
        o = c
        for b in range(C.bit_length() - 1):
            if (m >> b) & 1:
                o = o + (1 - 2 * lax.rem(c // (1 << b), 2)) * (1 << b)
        return o

    paced = G == 2 and C & (C - 1) == 0 and T > 1
    half = T // 2
    inner = tgt + lax.rem(c, T) // max(half, 1) == 1
    outer = jnp.logical_not(inner)
    mate = flip(half) if paced else c
    barrier = pltpu.get_barrier_semaphore()

    def greet(device, where=barrier):
        pl.semaphore_signal(where, inc=1, device_id=device, device_id_type=MESH)

    if paced:
        @pl.when(tgt != a)
        def _():
            for m in range(T, C):
                for s in range(G):
                    greet((flip(m), s))

        for m in range(half):
            for s in range(1 if m == 0 else 0, G):
                greet((flip(m), lax.rem(a + s, G)))

        @pl.when(inner)
        def _():
            greet((mate, a))
    else:
        for i in range(T):
            source = a * T + lax.rem(c + i, T)
            for s in range(1 if i == 0 else 0, G):
                greet((source, lax.rem(a + s, G)))

        @pl.when(tgt != a)
        def _():
            greet((a * T + lax.rem(c, T), a))

        for s in range(1, G):
            greet((c, lax.rem(a + s, G)))

    sys_copy = pltpu.make_async_copy(system, sysv, sys_sem)
    sys_copy.start()
    first_copy = pltpu.make_async_copy(first_in, first, first_sem)
    first_copy.start()
    img_copies = []
    for q in range(NC):
        for b in range(G):
            cp = pltpu.make_async_copy(
                image.at[pl.ds(b * KR + starts[q], sizes[q])],
                img.at[pl.ds(G * starts[q] + b * sizes[q], sizes[q])],
                img_sem.at[q, b],
            )
            cp.start()
            img_copies.append(cp)
    if paced:
        pl.semaphore_wait(barrier, C - T + G * half - 1 + jnp.where(inner, 0, 1))
    else:
        pl.semaphore_wait(barrier, C + G - 2 + jnp.where(tgt == a, 0, 1))

    def piece(q, o, k=0):
        return pltpu.make_async_remote_copy(
            src_ref=proj.at[0, o, 0, pl.ds(starts[q], sizes[q])],
            dst_ref=arr[q].at[slot],
            send_sem=send_sem.at[q, k],
            recv_sem=arr_sem.at[q],
            device_id=(o, tgt),
            device_id_type=MESH,
        )

    turn = TURN[:NC] if paced and NC == len(TURN) else (0,) * NC
    turns = max(turn) + 1
    AHEAD = 2 if paced else 0

    def send_self(q, k):
        @pl.when(tgt != a)
        def _():
            piece(q, c, k).start()

        @pl.when(tgt == a)
        def _():
            pltpu.make_async_copy(
                proj.at[0, c, 0, pl.ds(starts[q], sizes[q])], arr[q].at[slot], arr_sem.at[q]
            ).start()

    def send_plane(q):
        for m in range(half - 1, 0, -1):
            piece(q, flip(m), 1).start()
        send_self(q, 1)

    def send_half():
        for q in range(NC):
            for m in range(T - 1, half - 1, -1):
                piece(q, flip(m), 1).start()

    def send_ahead(q):
        if AHEAD and q < NC:
            @pl.when(tgt == G - 1)
            def _():
                for o in range(AHEAD):
                    piece(q, o).start()

    def send(q):
        send_ahead(q + 1)
        for m in range(T, C):
            o = flip(m)

            @pl.when((tgt != G - 1) | (o >= AHEAD))
            def _(o=o):
                piece(q, o).start()

    def sent_blocks(q, k, n):
        part = proj.at[0, pl.ds(0, n), 0, pl.ds(starts[q], sizes[q])]
        pltpu.make_async_copy(part, part, send_sem.at[q, k]).wait()

    def sent(q):
        sent_blocks(q, 0, C - T)

    def of_turn(k):
        return [q for q in range(NC) if turn[q] == k]

    if paced:
        send_ahead(0)
        for q in of_turn(0):
            send(q)
        if turns > 1:
            @pl.when(inner)
            def _():
                for k in range(1, turns):
                    for q in of_turn(k):
                        send(q)
        for q in range(NC):
            send_plane(q)

        @pl.when(outer)
        def _():
            greet((mate, a), up_sem)
    else:
        for q in range(NC):
            for i in range(1, C):
                piece(q, lax.rem(c + i, C)).start()
            send_self(q, 0)

    def meet():
        pl.semaphore_wait(up_sem, 1)

        @pl.when(inner)
        def _():
            greet((mate, a), up_sem)

        send_half()

    def take_turn(k):
        if k >= turns:
            return

        @pl.when(inner)
        def _():
            for q in of_turn(k - 1):
                sent(q)
            pl.semaphore_signal(go_sem.at[k - 1], inc=1, device_id=(mate, a), device_id_type=MESH)

        @pl.when(outer)
        def _():
            pl.semaphore_wait(go_sem.at[k - 1], 1)
            for q in of_turn(k):
                send(q)

    img[pl.ds(slices, PAD)] = jnp.ones((PAD, npix), jnp.bfloat16)
    R[pl.ds(0, PAD)] = jnp.ones((PAD, T * bins), jnp.bfloat16)
    sys_copy.wait()
    first_copy.wait()

    def build(i, carry):
        lane = lax.broadcasted_iota(jnp.int32, (W, pair * W), 1) // W
        cols = pl.ds(pl.multiple_of(i * pair * W, pair * W), pair * W)
        for g in range(blocks):
            x = [
                jnp.concatenate([sysv[g, i * pair + k, j] for k in range(pair)], axis=0)
                .astype(jnp.float32).T.astype(jnp.bfloat16)
                for j in range(2)
            ]
            f = jnp.full(lane.shape, first[g, i * pair], jnp.int32)
            for k in range(1, pair):
                f = jnp.where(lane == k, first[g, i * pair + k], f)
            second = jnp.where(f == ntiles - 1, 0, f + 1)
            for b in range(ntiles):
                m0, m1 = f == b, second == b
                for t in range(pair):
                    part = slice(t * W, (t + 1) * W)
                    tile = jnp.where(m0, x[0][part], jnp.where(m1, x[1][part], jnp.zeros((), jnp.bfloat16)))
                    A[pl.ds((g * pair + t) * bins + b * W, W), cols] = tile
        return carry

    lax.fori_loop(0, ptiles // pair, build, 0)
    if paced:
        meet()

    for cp in img_copies:
        cp.wait()

    def project(t, carry):
        m = A[pl.ds(pl.multiple_of(t * bins, bins), bins)]
        F[t] = lax.dot_general(img[...], m, NT, preferred_element_type=jnp.float32)
        return carry

    lax.fori_loop(0, T, project, 0)

    def residual_part(q):
        def body(t, carry):
            scale = 1.0 / F[t, pl.ds(slices, 8)][:1]
            for b in range(G):
                value = arr[q][b * T + t].astype(jnp.float32)
                f = F[t, pl.ds(G * starts[q] + b * sizes[q], sizes[q])]
                res = ((value - f) * scale).astype(jnp.bfloat16)
                R[
                    pl.ds(PAD + G * starts[q] + b * sizes[q], sizes[q]),
                    pl.ds(pl.multiple_of(t * bins, bins), bins),
                ] = res
                res_out[t, pl.ds(b * KR + starts[q], sizes[q])] = res
            return carry

        lax.fori_loop(0, T, body, 0)

    def back(lo, hi, g):
        return jnp.dot(
            R[pl.ds(lo, hi - lo)],
            A[:, pl.ds(pl.multiple_of(g * share, share), share)],
            preferred_element_type=jnp.float32,
        )

    def col_copy(s):
        g = lax.rem(a + s, G)
        return pltpu.make_async_remote_copy(
            src_ref=colp.at[g], dst_ref=crecv.at[s - 1], send_sem=csend_sem.at[s - 1],
            recv_sem=crecv_sem, device_id=(c, g), device_id_type=MESH,
        )

    def u_copy(q, s):
        g = lax.rem(a + s, G)
        return pltpu.make_async_remote_copy(
            src_ref=U[q].at[s - 1], dst_ref=urecv[q].at[s - 1],
            send_sem=usend_sem.at[q, s - 1], recv_sem=urecv_sem.at[q, s - 1],
            device_id=(c, g), device_id_type=MESH,
        )

    def unit_copy(q, s):
        g = lax.rem(a + s, G)
        return pltpu.make_async_remote_copy(
            src_ref=unit[q].at[s - 1], dst_ref=unitrecv[q].at[s - 1],
            send_sem=nsend_sem.at[q, s - 1], recv_sem=nrecv_sem.at[q, s - 1],
            device_id=(c, g), device_id_type=MESH,
        )

    def own_back(lo, hi):
        y = back(lo, hi, a)
        if lo == 0:
            colp[a] = y[:8]
            y = y[PAD:]
            lo = PAD
        own[pl.ds(lo - PAD, hi - lo)] = y

    def process(q):
        pltpu.make_async_copy(arr[q], arr[q], arr_sem.at[q]).wait()
        residual_part(q)
        lo = 0 if q == 0 else PAD + G * starts[q]
        hi = PAD + G * (starts[q] + sizes[q])
        for s in range(1, G):
            y = back(lo, hi, lax.rem(a + s, G))
            if q == 0:
                colp[lax.rem(a + s, G)] = y[:8]
                y = y[PAD:]
            top = jnp.maximum(jnp.max(jnp.abs(y), axis=0, keepdims=True), TINY)
            unit[q][s - 1] = top * (1.0 / STEPS)
            U[q][s - 1] = jnp.round(y * (STEPS / top)).astype(jnp.int32).astype(jnp.int16)
            unit_copy(q, s).start()
            u_copy(q, s).start()
            if q == 0:
                col_copy(s).start()
        late = max(NC - LATE, 0)
        if q < late:
            own_back(lo, hi)
        elif q == NC - 1:
            own_back(0 if late == 0 else PAD + G * starts[late], hi)

    def finish(q, own_inv):
        total = own[pl.ds(G * starts[q], G * sizes[q])]
        for s in range(1, G):
            u_copy(q, s).wait_recv()
            unit_copy(q, s).wait_recv()
            total = total + urecv[q][s - 1].astype(jnp.int32).astype(jnp.float32) * unitrecv[q][s - 1]
        mine = img[
            pl.ds(G * starts[q], G * sizes[q]), pl.ds(pl.multiple_of(a * share, share), share)
        ]
        new = mine.astype(jnp.float32) + total * own_inv
        for b in range(G):
            new_out[pl.ds(b * KR + starts[q], sizes[q])] = new[b * sizes[q] : (b + 1) * sizes[q]]

    take_turn(1)
    for q in range(NC):
        process(q)
        take_turn(q + 2)

    pltpu.make_async_copy(crecv, crecv, crecv_sem).wait()
    columns = colp[a][:1]
    for s in range(1, G):
        columns = columns + crecv[s - 1][:1]
    own_inv = 1.0 / columns
    for q in range(NC):
        finish(q, own_inv)

    for q in range(NC):
        if not paced:
            @pl.when(tgt == a)
            def _(q=q):
                sent_blocks(q, 0, C - 1)

            @pl.when(tgt != a)
            def _(q=q):
                sent_blocks(q, 0, C)

            continue
        if turn[q] == turns - 1:
            sent(q)
        else:
            @pl.when(outer)
            def _(q=q):
                sent(q)

        @pl.when(tgt == a)
        def _(q=q):
            sent_blocks(q, 1, T - 1)

        @pl.when(tgt != a)
        def _(q=q):
            sent_blocks(q, 1, T)

    for s in range(1, G):
        col_copy(s).wait_send()
    for q in range(NC):
        for s in range(1, G):
            u_copy(q, s).wait_send()
            unit_copy(q, s).wait_send()


def put_out(new_in, res_in, new_out, res_out, sem):
    copies = []
    for i, (src, dst) in enumerate(((new_in, new_out), (res_in, res_out))):
        n = src.shape[0] // PUTS
        for k in range(PUTS):
            part = pl.ds(k * n, n)
            copies.append(pltpu.make_async_copy(src.at[part], dst.at[part], sem.at[i * PUTS + k]))
    for cp in copies:
        cp.start()
    for cp in copies:
        cp.wait()


def chunk_sizes(rows):
    unit = max(16, rows // sum(SPLIT))
    sizes = [n * unit for n in SPLIT]
    if sum(sizes) == rows:
        return sizes
    return [16] * (rows // 16) if rows % 16 == 0 else [rows]


def on_device(C, G, projections, start_image, system, first_tile):
    T = C // G
    KR = projections.shape[3]
    sizes = chunk_sizes(KR)
    NC = len(sizes)
    slices, npix = start_image.shape
    bins = projections.shape[4]
    share = npix // G
    bf16, f32 = jnp.bfloat16, jnp.float32
    dma = pltpu.SemaphoreType.DMA
    out_bytes = slices * share * 4 + T * slices * bins * 2
    new_image, residual = pl.pallas_call(
        functools.partial(kernel, C, G, sizes),
        out_shape=(
            pltpu.VMEM((slices, share), f32),
            pltpu.VMEM((T, slices, bins), bf16),
        ),
        in_specs=[pl.BlockSpec(memory_space=pltpu.HBM)] * 4,
        out_specs=(pl.BlockSpec(memory_space=pltpu.VMEM),) * 2,
        scratch_shapes=[
            pltpu.SMEM(first_tile.shape, jnp.int32),
            pltpu.VMEM((slices + PAD, npix), bf16),
            pltpu.VMEM(system.shape, bf16),
            pltpu.VMEM((T * bins, npix), bf16),
            pltpu.VMEM((T, slices + PAD, bins), f32),
            pltpu.VMEM((slices + PAD, T * bins), bf16),
            [pltpu.VMEM((C, n, bins), bf16) for n in sizes],
            [pltpu.VMEM((G - 1, G * n, share), jnp.int16) for n in sizes],
            [pltpu.VMEM((G - 1, 1, share), f32) for n in sizes],
            pltpu.VMEM((slices, share), f32),
            [pltpu.VMEM((G - 1, G * n, share), jnp.int16) for n in sizes],
            [pltpu.VMEM((G - 1, 1, share), f32) for n in sizes],
            pltpu.VMEM((G, 8, share), f32),
            pltpu.VMEM((G - 1, 8, share), f32),
            dma,
            dma((NC, G)),
            dma,
            dma((NC, 2)),
            dma((NC,)),
            pltpu.SemaphoreType.REGULAR((max(NC, 2),)),
            pltpu.SemaphoreType.REGULAR,
            dma((NC, G - 1)),
            dma((NC, G - 1)),
            dma((NC, G - 1)),
            dma((NC, G - 1)),
            dma((G - 1,)),
            dma,
        ],
        compiler_params=pltpu.CompilerParams(
            collective_id=0, has_side_effects=True, vmem_limit_bytes=VMEM_BYTES - out_bytes
        ),
    )(first_tile, projections, start_image, system)
    return pl.pallas_call(
        put_out,
        out_shape=(
            jax.ShapeDtypeStruct(new_image.shape, f32),
            jax.ShapeDtypeStruct(residual.shape, bf16),
        ),
        in_specs=[pl.BlockSpec(memory_space=pl.ANY)] * 2,
        out_specs=(pl.BlockSpec(memory_space=pl.ANY),) * 2,
        scratch_shapes=[dma((2 * PUTS,))],
        compiler_params=pltpu.CompilerParams(vmem_limit_bytes=1 << 20),
    )(new_image, residual)


def solution(mesh):
    in_specs = (
        P("cuts", None, "ang", None, None),
        P("cuts", None),
        P("ang", None, None, None, None),
        P("ang", None),
    )
    out_specs = (P("cuts", "ang"), P("ang", "cuts", None))
    return jax.shard_map(
        functools.partial(on_device, mesh.shape["cuts"], mesh.shape["ang"]),
        mesh=mesh, in_specs=in_specs, out_specs=out_specs, check_vma=False,
    )
```

```python
import functools

import jax
import jax.numpy as jnp
from jax import lax
from jax.experimental import pallas as pl
from jax.experimental.pallas import tpu as pltpu
from jax.sharding import PartitionSpec as P

MESH = pl.DeviceIdType.MESH
NT = (((1,), (1,)), ((), ()))
SPLIT = (2, 2, 2, 2)
TURN = (0, 1, 2, 2)
LATE = 2
PUTS = 2
PAD = 16
STEPS = 32767.0
TINY = 1e-30
VMEM_BYTES = 67043328


def kernel(
    C, G, sizes, first_in, proj, image, system, new_out, res_out,
    first, img, sysv, A, F, R, arr, U, unit, own, urecv, unitrecv, colp, crecv,
    first_sem, img_sem, sys_sem, send_sem, arr_sem, go_sem, up_sem,
    usend_sem, urecv_sem, nsend_sem, nrecv_sem, csend_sem, crecv_sem,
):
    c = lax.axis_index("cuts")
    a = lax.axis_index("ang")
    T = C // G
    blocks, ptiles, _, W, PW = system.shape
    KR = proj.shape[3]
    NC = len(sizes)
    starts = [sum(sizes[:q]) for q in range(NC)]
    slices, npix = image.shape
    share = npix // G
    bins = proj.shape[4]
    ntiles = bins // W
    pair = PW // W

    tgt = c // T
    slot = a * T + lax.rem(c, T)

    def flip(m):
        o = c
        for b in range(C.bit_length() - 1):
            if (m >> b) & 1:
                o = o + (1 - 2 * lax.rem(c // (1 << b), 2)) * (1 << b)
        return o

    paced = G == 2 and C & (C - 1) == 0 and T > 1
    half = T // 2
    inner = tgt + lax.rem(c, T) // max(half, 1) == 1
    outer = jnp.logical_not(inner)
    mate = flip(half) if paced else c
    barrier = pltpu.get_barrier_semaphore()

    def greet(device, where=barrier):
        pl.semaphore_signal(where, inc=1, device_id=device, device_id_type=MESH)

    if paced:
        @pl.when(tgt != a)
        def _():
            for m in range(T, C):
                for s in range(G):
                    greet((flip(m), s))

        for m in range(half):
            for s in range(1 if m == 0 else 0, G):
                greet((flip(m), lax.rem(a + s, G)))

        @pl.when(inner)
        def _():
            greet((mate, a))
    else:
        for i in range(T):
            source = a * T + lax.rem(c + i, T)
            for s in range(1 if i == 0 else 0, G):
                greet((source, lax.rem(a + s, G)))

        @pl.when(tgt != a)
        def _():
            greet((a * T + lax.rem(c, T), a))

        for s in range(1, G):
            greet((c, lax.rem(a + s, G)))

    sys_copy = pltpu.make_async_copy(system, sysv, sys_sem)
    sys_copy.start()
    first_copy = pltpu.make_async_copy(first_in, first, first_sem)
    first_copy.start()
    img_copies = []
    for q in range(NC):
        for b in range(G):
            cp = pltpu.make_async_copy(
                image.at[pl.ds(b * KR + starts[q], sizes[q])],
                img.at[pl.ds(G * starts[q] + b * sizes[q], sizes[q])],
                img_sem.at[q, b],
            )
            cp.start()
            img_copies.append(cp)
    if paced:
        pl.semaphore_wait(barrier, C - T + G * half - 1 + jnp.where(inner, 0, 1))
    else:
        pl.semaphore_wait(barrier, C + G - 2 + jnp.where(tgt == a, 0, 1))

    def piece(q, o, k=0):
        return pltpu.make_async_remote_copy(
            src_ref=proj.at[0, o, 0, pl.ds(starts[q], sizes[q])],
            dst_ref=arr[q].at[slot],
            send_sem=send_sem.at[q, k],
            recv_sem=arr_sem.at[q],
            device_id=(o, tgt),
            device_id_type=MESH,
        )

    turn = TURN[:NC] if paced and NC == len(TURN) else (0,) * NC
    turns = max(turn) + 1
    AHEAD = 2 if paced else 0
    CROSS = sorted(range(T, C), key=lambda m: (m & half, -(m & (half // 2)), m))

    def send_self(q, k):
        @pl.when(tgt != a)
        def _():
            piece(q, c, k).start()

        @pl.when(tgt == a)
        def _():
            pltpu.make_async_copy(
                proj.at[0, c, 0, pl.ds(starts[q], sizes[q])], arr[q].at[slot], arr_sem.at[q]
            ).start()

    def send_plane(q):
        for m in range(half - 1, 0, -1):
            piece(q, flip(m), 1).start()
        send_self(q, 1)

    def send_half():
        for q in range(NC):
            for m in range(T - 1, half - 1, -1):
                piece(q, flip(m), 1).start()

    def send_ahead(q):
        if AHEAD and q < NC:
            @pl.when(tgt == G - 1)
            def _():
                for o in range(AHEAD):
                    piece(q, o).start()

    def send(q):
        send_ahead(q + 1)
        for m in CROSS:
            o = flip(m)

            @pl.when((tgt != G - 1) | (o >= AHEAD))
            def _(o=o):
                piece(q, o).start()

    def sent_blocks(q, k, n):
        part = proj.at[0, pl.ds(0, n), 0, pl.ds(starts[q], sizes[q])]
        pltpu.make_async_copy(part, part, send_sem.at[q, k]).wait()

    def sent(q):
        sent_blocks(q, 0, C - T)

    def of_turn(k):
        return [q for q in range(NC) if turn[q] == k]

    if paced:
        send_ahead(0)
        for q in of_turn(0):
            send(q)
        if turns > 1:
            @pl.when(inner)
            def _():
                for k in range(1, turns):
                    for q in of_turn(k):
                        send(q)
        for q in range(NC):
            send_plane(q)

        @pl.when(outer)
        def _():
            greet((mate, a), up_sem)
    else:
        for q in range(NC):
            for i in range(1, C):
                piece(q, lax.rem(c + i, C)).start()
            send_self(q, 0)

    def meet():
        pl.semaphore_wait(up_sem, 1)

        @pl.when(inner)
        def _():
            greet((mate, a), up_sem)

        send_half()

    def take_turn(k):
        if k >= turns:
            return

        @pl.when(inner)
        def _():
            for q in of_turn(k - 1):
                sent(q)
            pl.semaphore_signal(go_sem.at[k - 1], inc=1, device_id=(mate, a), device_id_type=MESH)

        @pl.when(outer)
        def _():
            pl.semaphore_wait(go_sem.at[k - 1], 1)
            for q in of_turn(k):
                send(q)

    img[pl.ds(slices, PAD)] = jnp.ones((PAD, npix), jnp.bfloat16)
    R[pl.ds(0, PAD)] = jnp.ones((PAD, T * bins), jnp.bfloat16)
    sys_copy.wait()
    first_copy.wait()

    def build(i, carry):
        lane = lax.broadcasted_iota(jnp.int32, (W, pair * W), 1) // W
        cols = pl.ds(pl.multiple_of(i * pair * W, pair * W), pair * W)
        for g in range(blocks):
            x = [
                jnp.concatenate([sysv[g, i * pair + k, j] for k in range(pair)], axis=0)
                .astype(jnp.float32).T.astype(jnp.bfloat16)
                for j in range(2)
            ]
            f = jnp.full(lane.shape, first[g, i * pair], jnp.int32)
            for k in range(1, pair):
                f = jnp.where(lane == k, first[g, i * pair + k], f)
            second = jnp.where(f == ntiles - 1, 0, f + 1)
            for b in range(ntiles):
                m0, m1 = f == b, second == b
                for t in range(pair):
                    part = slice(t * W, (t + 1) * W)
                    tile = jnp.where(m0, x[0][part], jnp.where(m1, x[1][part], jnp.zeros((), jnp.bfloat16)))
                    A[pl.ds((g * pair + t) * bins + b * W, W), cols] = tile
        return carry

    lax.fori_loop(0, ptiles // pair, build, 0)
    if paced:
        meet()

    for cp in img_copies:
        cp.wait()

    def project(t, carry):
        m = A[pl.ds(pl.multiple_of(t * bins, bins), bins)]
        F[t] = lax.dot_general(img[...], m, NT, preferred_element_type=jnp.float32)
        return carry

    lax.fori_loop(0, T, project, 0)

    def residual_part(q):
        def body(t, carry):
            scale = 1.0 / F[t, pl.ds(slices, 8)][:1]
            for b in range(G):
                value = arr[q][b * T + t].astype(jnp.float32)
                f = F[t, pl.ds(G * starts[q] + b * sizes[q], sizes[q])]
                res = ((value - f) * scale).astype(jnp.bfloat16)
                R[
                    pl.ds(PAD + G * starts[q] + b * sizes[q], sizes[q]),
                    pl.ds(pl.multiple_of(t * bins, bins), bins),
                ] = res
                res_out[t, pl.ds(b * KR + starts[q], sizes[q])] = res
            return carry

        lax.fori_loop(0, T, body, 0)

    def back(lo, hi, g):
        return jnp.dot(
            R[pl.ds(lo, hi - lo)],
            A[:, pl.ds(pl.multiple_of(g * share, share), share)],
            preferred_element_type=jnp.float32,
        )

    def col_copy(s):
        g = lax.rem(a + s, G)
        return pltpu.make_async_remote_copy(
            src_ref=colp.at[g], dst_ref=crecv.at[s - 1], send_sem=csend_sem.at[s - 1],
            recv_sem=crecv_sem, device_id=(c, g), device_id_type=MESH,
        )

    def u_copy(q, s):
        g = lax.rem(a + s, G)
        return pltpu.make_async_remote_copy(
            src_ref=U[q].at[s - 1], dst_ref=urecv[q].at[s - 1],
            send_sem=usend_sem.at[q, s - 1], recv_sem=urecv_sem.at[q, s - 1],
            device_id=(c, g), device_id_type=MESH,
        )

    def unit_copy(q, s):
        g = lax.rem(a + s, G)
        return pltpu.make_async_remote_copy(
            src_ref=unit[q].at[s - 1], dst_ref=unitrecv[q].at[s - 1],
            send_sem=nsend_sem.at[q, s - 1], recv_sem=nrecv_sem.at[q, s - 1],
            device_id=(c, g), device_id_type=MESH,
        )

    def own_back(lo, hi):
        y = back(lo, hi, a)
        if lo == 0:
            colp[a] = y[:8]
            y = y[PAD:]
            lo = PAD
        own[pl.ds(lo - PAD, hi - lo)] = y

    def process(q):
        pltpu.make_async_copy(arr[q], arr[q], arr_sem.at[q]).wait()
        residual_part(q)
        lo = 0 if q == 0 else PAD + G * starts[q]
        hi = PAD + G * (starts[q] + sizes[q])
        for s in range(1, G):
            y = back(lo, hi, lax.rem(a + s, G))
            if q == 0:
                colp[lax.rem(a + s, G)] = y[:8]
                y = y[PAD:]
            top = jnp.maximum(jnp.max(jnp.abs(y), axis=0, keepdims=True), TINY)
            unit[q][s - 1] = top * (1.0 / STEPS)
            U[q][s - 1] = jnp.round(y * (STEPS / top)).astype(jnp.int32).astype(jnp.int16)
            unit_copy(q, s).start()
            u_copy(q, s).start()
            if q == 0:
                col_copy(s).start()
        late = max(NC - LATE, 0)
        if q < late:
            own_back(lo, hi)
        elif q == NC - 1:
            own_back(0 if late == 0 else PAD + G * starts[late], hi)

    def finish(q, own_inv):
        total = own[pl.ds(G * starts[q], G * sizes[q])]
        for s in range(1, G):
            u_copy(q, s).wait_recv()
            unit_copy(q, s).wait_recv()
            total = total + urecv[q][s - 1].astype(jnp.int32).astype(jnp.float32) * unitrecv[q][s - 1]
        mine = img[
            pl.ds(G * starts[q], G * sizes[q]), pl.ds(pl.multiple_of(a * share, share), share)
        ]
        new = mine.astype(jnp.float32) + total * own_inv
        for b in range(G):
            new_out[pl.ds(b * KR + starts[q], sizes[q])] = new[b * sizes[q] : (b + 1) * sizes[q]]

    take_turn(1)
    for q in range(NC):
        process(q)
        take_turn(q + 2)

    pltpu.make_async_copy(crecv, crecv, crecv_sem).wait()
    columns = colp[a][:1]
    for s in range(1, G):
        columns = columns + crecv[s - 1][:1]
    own_inv = 1.0 / columns
    for q in range(NC - 1):
        finish(q, own_inv)

    for q in range(NC):
        if not paced:
            @pl.when(tgt == a)
            def _(q=q):
                sent_blocks(q, 0, C - 1)

            @pl.when(tgt != a)
            def _(q=q):
                sent_blocks(q, 0, C)

            continue
        if turn[q] == turns - 1:
            sent(q)
        else:
            @pl.when(outer)
            def _(q=q):
                sent(q)

        @pl.when(tgt == a)
        def _(q=q):
            sent_blocks(q, 1, T - 1)

        @pl.when(tgt != a)
        def _(q=q):
            sent_blocks(q, 1, T)

    for s in range(1, G):
        col_copy(s).wait_send()
    for q in range(NC):
        if q == NC - 1:
            finish(q, own_inv)
        for s in range(1, G):
            u_copy(q, s).wait_send()
            unit_copy(q, s).wait_send()


def put_out(new_in, res_in, new_out, res_out, sem):
    copies = []
    for i, (src, dst) in enumerate(((new_in, new_out), (res_in, res_out))):
        n = src.shape[0] // PUTS
        for k in range(PUTS):
            part = pl.ds(k * n, n)
            copies.append(pltpu.make_async_copy(src.at[part], dst.at[part], sem.at[i * PUTS + k]))
    for cp in copies:
        cp.start()
    for cp in copies:
        cp.wait()


def chunk_sizes(rows):
    unit = max(16, rows // sum(SPLIT))
    sizes = [n * unit for n in SPLIT]
    if sum(sizes) == rows:
        return sizes
    return [16] * (rows // 16) if rows % 16 == 0 else [rows]


def on_device(C, G, projections, start_image, system, first_tile):
    T = C // G
    KR = projections.shape[3]
    sizes = chunk_sizes(KR)
    NC = len(sizes)
    slices, npix = start_image.shape
    bins = projections.shape[4]
    share = npix // G
    bf16, f32 = jnp.bfloat16, jnp.float32
    dma = pltpu.SemaphoreType.DMA
    out_bytes = slices * share * 4 + T * slices * bins * 2
    new_image, residual = pl.pallas_call(
        functools.partial(kernel, C, G, sizes),
        out_shape=(
            pltpu.VMEM((slices, share), f32),
            pltpu.VMEM((T, slices, bins), bf16),
        ),
        in_specs=[pl.BlockSpec(memory_space=pltpu.HBM)] * 4,
        out_specs=(pl.BlockSpec(memory_space=pltpu.VMEM),) * 2,
        scratch_shapes=[
            pltpu.SMEM(first_tile.shape, jnp.int32),
            pltpu.VMEM((slices + PAD, npix), bf16),
            pltpu.VMEM(system.shape, bf16),
            pltpu.VMEM((T * bins, npix), bf16),
            pltpu.VMEM((T, slices + PAD, bins), f32),
            pltpu.VMEM((slices + PAD, T * bins), bf16),
            [pltpu.VMEM((C, n, bins), bf16) for n in sizes],
            [pltpu.VMEM((G - 1, G * n, share), jnp.int16) for n in sizes],
            [pltpu.VMEM((G - 1, 1, share), f32) for n in sizes],
            pltpu.VMEM((slices, share), f32),
            [pltpu.VMEM((G - 1, G * n, share), jnp.int16) for n in sizes],
            [pltpu.VMEM((G - 1, 1, share), f32) for n in sizes],
            pltpu.VMEM((G, 8, share), f32),
            pltpu.VMEM((G - 1, 8, share), f32),
            dma,
            dma((NC, G)),
            dma,
            dma((NC, 2)),
            dma((NC,)),
            pltpu.SemaphoreType.REGULAR((max(NC, 2),)),
            pltpu.SemaphoreType.REGULAR,
            dma((NC, G - 1)),
            dma((NC, G - 1)),
            dma((NC, G - 1)),
            dma((NC, G - 1)),
            dma((G - 1,)),
            dma,
        ],
        compiler_params=pltpu.CompilerParams(
            collective_id=0, has_side_effects=True, vmem_limit_bytes=VMEM_BYTES - out_bytes
        ),
    )(first_tile, projections, start_image, system)
    return pl.pallas_call(
        put_out,
        out_shape=(
            jax.ShapeDtypeStruct(new_image.shape, f32),
            jax.ShapeDtypeStruct(residual.shape, bf16),
        ),
        in_specs=[pl.BlockSpec(memory_space=pl.ANY)] * 2,
        out_specs=(pl.BlockSpec(memory_space=pl.ANY),) * 2,
        scratch_shapes=[dma((2 * PUTS,))],
        compiler_params=pltpu.CompilerParams(vmem_limit_bytes=1 << 20),
    )(new_image, residual)


def solution(mesh):
    in_specs = (
        P("cuts", None, "ang", None, None),
        P("cuts", None),
        P("ang", None, None, None, None),
        P("ang", None),
    )
    out_specs = (P("cuts", "ang"), P("ang", "cuts", None))
    return jax.shard_map(
        functools.partial(on_device, mesh.shape["cuts"], mesh.shape["ang"]),
        mesh=mesh, in_specs=in_specs, out_specs=out_specs, check_vma=False,
    )
```

```python
import functools

import jax
import jax.numpy as jnp
from jax import lax
from jax.experimental import pallas as pl
from jax.experimental.pallas import tpu as pltpu
from jax.sharding import PartitionSpec as P

MESH = pl.DeviceIdType.MESH
NT = (((1,), (1,)), ((), ()))
SPLIT = (2, 2, 2, 2)
TURN = (0, 1, 2, 2)
LATE = 2
PUTS = 2
PAD = 16
STEPS = 32767.0
TINY = 1e-30
ROUND = 12582912.0
VMEM_BYTES = 67043328


def kernel(
    C, G, sizes, first_in, proj, image, system, new_out, res_out,
    held, first, img, sysv, A, F, R, arr, U, unit, own, urecv, unitrecv, colp, crecv,
    held_sem, first_sem, img_sem, sys_sem, send_sem, arr_sem, go_sem, up_sem,
    usend_sem, urecv_sem, nsend_sem, nrecv_sem, csend_sem, crecv_sem,
):
    c = lax.axis_index("cuts")
    a = lax.axis_index("ang")
    T = C // G
    blocks, ptiles, _, W, PW = system.shape
    KR = proj.shape[3]
    NC = len(sizes)
    starts = [sum(sizes[:q]) for q in range(NC)]
    slices, npix = image.shape
    share = npix // G
    bins = proj.shape[4]
    ntiles = bins // W
    pair = PW // W

    tgt = c // T
    slot = a * T + lax.rem(c, T)

    def flip(m):
        o = c
        for b in range(C.bit_length() - 1):
            if (m >> b) & 1:
                o = o + (1 - 2 * lax.rem(c // (1 << b), 2)) * (1 << b)
        return o

    paced = G == 2 and C & (C - 1) == 0 and T > 1
    held_copy = pltpu.make_async_copy(proj.at[0, :, 0], held, held_sem)
    held_copy.start()
    half = T // 2
    inner = tgt + lax.rem(c, T) // max(half, 1) == 1
    outer = jnp.logical_not(inner)
    mate = flip(half) if paced else c
    barrier = pltpu.get_barrier_semaphore()

    def greet(device, where=barrier):
        pl.semaphore_signal(where, inc=1, device_id=device, device_id_type=MESH)

    if paced:
        @pl.when(tgt != a)
        def _():
            for m in range(T, C):
                for s in range(G):
                    greet((flip(m), s))

        for m in range(half):
            for s in range(1 if m == 0 else 0, G):
                greet((flip(m), lax.rem(a + s, G)))

        @pl.when(inner)
        def _():
            greet((mate, a))
    else:
        for i in range(T):
            source = a * T + lax.rem(c + i, T)
            for s in range(1 if i == 0 else 0, G):
                greet((source, lax.rem(a + s, G)))

        @pl.when(tgt != a)
        def _():
            greet((a * T + lax.rem(c, T), a))

        for s in range(1, G):
            greet((c, lax.rem(a + s, G)))

    sys_copy = pltpu.make_async_copy(system, sysv, sys_sem)
    sys_copy.start()
    first_copy = pltpu.make_async_copy(first_in, first, first_sem)
    first_copy.start()
    img_copies = []
    for q in range(NC):
        for b in range(G):
            cp = pltpu.make_async_copy(
                image.at[pl.ds(b * KR + starts[q], sizes[q])],
                img.at[pl.ds(G * starts[q] + b * sizes[q], sizes[q])],
                img_sem.at[q, b],
            )
            cp.start()
            img_copies.append(cp)
    if paced:
        pl.semaphore_wait(barrier, C - T + G * half - 1 + jnp.where(inner, 0, 1))
    else:
        pl.semaphore_wait(barrier, C + G - 2 + jnp.where(tgt == a, 0, 1))

    held_copy.wait()

    def piece(q, o, k=0):
        return pltpu.make_async_remote_copy(
            src_ref=held.at[o, pl.ds(starts[q], sizes[q])],
            dst_ref=arr[q].at[slot],
            send_sem=send_sem.at[q, k],
            recv_sem=arr_sem.at[q],
            device_id=(o, tgt),
            device_id_type=MESH,
        )

    turn = TURN[:NC] if paced and NC == len(TURN) else (0,) * NC
    turns = max(turn) + 1
    AHEAD = 2 if paced else 0
    CROSS = sorted(range(T, C), key=lambda m: (m & half, -(m & (half // 2)), m))

    def send_self(q, k):
        @pl.when(tgt != a)
        def _():
            piece(q, c, k).start()

        @pl.when(tgt == a)
        def _():
            pltpu.make_async_copy(
                held.at[c, pl.ds(starts[q], sizes[q])], arr[q].at[slot], arr_sem.at[q]
            ).start()

    def send_plane(q):
        for m in range(half - 1, 0, -1):
            piece(q, flip(m), 1).start()
        send_self(q, 1)

    def send_half():
        for q in range(NC):
            for m in range(T - 1, half - 1, -1):
                piece(q, flip(m), 1).start()

    def send_ahead(q):
        if AHEAD and q < NC:
            @pl.when(tgt == G - 1)
            def _():
                for o in range(AHEAD):
                    piece(q, o).start()

    def send(q):
        send_ahead(q + 1)
        for m in CROSS:
            o = flip(m)

            @pl.when((tgt != G - 1) | (o >= AHEAD))
            def _(o=o):
                piece(q, o).start()

    def sent_blocks(q, k, n):
        part = held.at[pl.ds(0, n), pl.ds(starts[q], sizes[q])]
        pltpu.make_async_copy(part, part, send_sem.at[q, k]).wait()

    def sent(q):
        sent_blocks(q, 0, C - T)

    def of_turn(k):
        return [q for q in range(NC) if turn[q] == k]

    if paced:
        send_ahead(0)
        for q in of_turn(0):
            send(q)
        if turns > 1:
            @pl.when(inner)
            def _():
                for k in range(1, turns):
                    for q in of_turn(k):
                        send(q)
        for q in range(NC):
            send_plane(q)

        @pl.when(outer)
        def _():
            greet((mate, a), up_sem)
    else:
        for q in range(NC):
            for i in range(1, C):
                piece(q, lax.rem(c + i, C)).start()
            send_self(q, 0)

    def meet():
        pl.semaphore_wait(up_sem, 1)

        @pl.when(inner)
        def _():
            greet((mate, a), up_sem)

        send_half()

    def take_turn(k):
        if k >= turns:
            return

        @pl.when(inner)
        def _():
            for q in of_turn(k - 1):
                sent(q)
            pl.semaphore_signal(go_sem.at[k - 1], inc=1, device_id=(mate, a), device_id_type=MESH)

        @pl.when(outer)
        def _():
            pl.semaphore_wait(go_sem.at[k - 1], 1)
            for q in of_turn(k):
                send(q)

    img[pl.ds(slices, PAD)] = jnp.ones((PAD, npix), jnp.bfloat16)
    R[pl.ds(0, PAD)] = jnp.ones((PAD, T * bins), jnp.bfloat16)
    sys_copy.wait()
    first_copy.wait()

    def build(i, carry):
        lane = lax.broadcasted_iota(jnp.int32, (W, pair * W), 1) // W
        cols = pl.ds(pl.multiple_of(i * pair * W, pair * W), pair * W)
        for g in range(blocks):
            x = [
                jnp.concatenate([sysv[g, i * pair + k, j] for k in range(pair)], axis=0)
                .astype(jnp.float32).T.astype(jnp.bfloat16)
                for j in range(2)
            ]
            f = jnp.full(lane.shape, first[g, i * pair], jnp.int32)
            for k in range(1, pair):
                f = jnp.where(lane == k, first[g, i * pair + k], f)
            second = jnp.where(f == ntiles - 1, 0, f + 1)
            for b in range(ntiles):
                m0, m1 = f == b, second == b
                for t in range(pair):
                    part = slice(t * W, (t + 1) * W)
                    tile = jnp.where(m0, x[0][part], jnp.where(m1, x[1][part], jnp.zeros((), jnp.bfloat16)))
                    A[pl.ds((g * pair + t) * bins + b * W, W), cols] = tile
        return carry

    lax.fori_loop(0, ptiles // pair, build, 0)
    if paced:
        meet()

    for cp in img_copies:
        cp.wait()

    def project(t, carry):
        m = A[pl.ds(pl.multiple_of(t * bins, bins), bins)]
        F[t] = lax.dot_general(img[...], m, NT, preferred_element_type=jnp.float32)
        return carry

    lax.fori_loop(0, T, project, 0)

    def residual_part(q):
        def body(t, carry):
            scale = 1.0 / F[t, pl.ds(slices, 8)][:1]
            for b in range(G):
                value = arr[q][b * T + t].astype(jnp.float32)
                f = F[t, pl.ds(G * starts[q] + b * sizes[q], sizes[q])]
                res = ((value - f) * scale).astype(jnp.bfloat16)
                R[
                    pl.ds(PAD + G * starts[q] + b * sizes[q], sizes[q]),
                    pl.ds(pl.multiple_of(t * bins, bins), bins),
                ] = res
                res_out[t, pl.ds(b * KR + starts[q], sizes[q])] = res
            return carry

        lax.fori_loop(0, T, body, 0)

    def back(lo, hi, g):
        return jnp.dot(
            R[pl.ds(lo, hi - lo)],
            A[:, pl.ds(pl.multiple_of(g * share, share), share)],
            preferred_element_type=jnp.float32,
        )

    def col_copy(s):
        g = lax.rem(a + s, G)
        return pltpu.make_async_remote_copy(
            src_ref=colp.at[g], dst_ref=crecv.at[s - 1], send_sem=csend_sem.at[s - 1],
            recv_sem=crecv_sem, device_id=(c, g), device_id_type=MESH,
        )

    def u_copy(q, s):
        g = lax.rem(a + s, G)
        return pltpu.make_async_remote_copy(
            src_ref=U[q].at[s - 1], dst_ref=urecv[q].at[s - 1],
            send_sem=usend_sem.at[q, s - 1], recv_sem=urecv_sem.at[q, s - 1],
            device_id=(c, g), device_id_type=MESH,
        )

    def unit_copy(q, s):
        g = lax.rem(a + s, G)
        return pltpu.make_async_remote_copy(
            src_ref=unit[q].at[s - 1], dst_ref=unitrecv[q].at[s - 1],
            send_sem=nsend_sem.at[q, s - 1], recv_sem=nrecv_sem.at[q, s - 1],
            device_id=(c, g), device_id_type=MESH,
        )

    def own_back(lo, hi):
        y = back(lo, hi, a)
        if lo == 0:
            colp[a] = y[:8]
            y = y[PAD:]
            lo = PAD
        own[pl.ds(lo - PAD, hi - lo)] = y

    def process(q):
        pltpu.make_async_copy(arr[q], arr[q], arr_sem.at[q]).wait()
        residual_part(q)
        lo = 0 if q == 0 else PAD + G * starts[q]
        hi = PAD + G * (starts[q] + sizes[q])
        for s in range(1, G):
            y = back(lo, hi, lax.rem(a + s, G))
            if q == 0:
                colp[lax.rem(a + s, G)] = y[:8]
                y = y[PAD:]
            top = jnp.maximum(jnp.max(jnp.abs(y), axis=0, keepdims=True), TINY)
            unit[q][s - 1] = top * (1.0 / STEPS)
            U[q][s - 1] = ((y * (STEPS / top) + ROUND) - ROUND).astype(jnp.int32).astype(jnp.int16)
            unit_copy(q, s).start()
            u_copy(q, s).start()
            if q == 0:
                col_copy(s).start()
        late = max(NC - LATE, 0)
        if q < late:
            own_back(lo, hi)
        elif q == NC - 1:
            own_back(0 if late == 0 else PAD + G * starts[late], hi)

    def prepare(own_inv):
        mine = img[pl.ds(0, slices), pl.ds(pl.multiple_of(a * share, share), share)]
        own[...] = mine.astype(jnp.float32) + own[...] * own_inv

    def finish(q, own_inv):
        new = own[pl.ds(G * starts[q], G * sizes[q])]
        for s in range(1, G):
            unit_copy(q, s).wait_recv()
            scale = unitrecv[q][s - 1] * own_inv
            u_copy(q, s).wait_recv()
            new = new + urecv[q][s - 1].astype(jnp.int32).astype(jnp.float32) * scale
        for b in range(G):
            new_out[pl.ds(b * KR + starts[q], sizes[q])] = new[b * sizes[q] : (b + 1) * sizes[q]]

    take_turn(1)
    for q in range(NC):
        process(q)
        take_turn(q + 2)

    pltpu.make_async_copy(crecv, crecv, crecv_sem).wait()
    columns = colp[a][:1]
    for s in range(1, G):
        columns = columns + crecv[s - 1][:1]
    own_inv = 1.0 / columns
    prepare(own_inv)
    for q in range(NC - 1):
        finish(q, own_inv)

    for q in range(NC):
        if not paced:
            @pl.when(tgt == a)
            def _(q=q):
                sent_blocks(q, 0, C - 1)

            @pl.when(tgt != a)
            def _(q=q):
                sent_blocks(q, 0, C)

            continue
        if turn[q] == turns - 1:
            sent(q)
        else:
            @pl.when(outer)
            def _(q=q):
                sent(q)

        @pl.when(tgt == a)
        def _(q=q):
            sent_blocks(q, 1, T - 1)

        @pl.when(tgt != a)
        def _(q=q):
            sent_blocks(q, 1, T)

    for s in range(1, G):
        col_copy(s).wait_send()
    for q in range(NC):
        if q == NC - 1:
            finish(q, own_inv)
        for s in range(1, G):
            u_copy(q, s).wait_send()
            unit_copy(q, s).wait_send()


def put_out(new_in, res_in, new_out, res_out, sem):
    copies = []
    for i, (src, dst) in enumerate(((new_in, new_out), (res_in, res_out))):
        n = src.shape[0] // PUTS
        for k in range(PUTS):
            part = pl.ds(k * n, n)
            copies.append(pltpu.make_async_copy(src.at[part], dst.at[part], sem.at[i * PUTS + k]))
    for cp in copies:
        cp.start()
    for cp in copies:
        cp.wait()


def chunk_sizes(rows):
    unit = max(16, rows // sum(SPLIT))
    sizes = [n * unit for n in SPLIT]
    if sum(sizes) == rows:
        return sizes
    return [16] * (rows // 16) if rows % 16 == 0 else [rows]


def on_device(C, G, projections, start_image, system, first_tile):
    T = C // G
    KR = projections.shape[3]
    sizes = chunk_sizes(KR)
    NC = len(sizes)
    slices, npix = start_image.shape
    bins = projections.shape[4]
    share = npix // G
    bf16, f32 = jnp.bfloat16, jnp.float32
    dma = pltpu.SemaphoreType.DMA
    out_bytes = slices * share * 4 + T * slices * bins * 2
    new_image, residual = pl.pallas_call(
        functools.partial(kernel, C, G, sizes),
        out_shape=(
            pltpu.VMEM((slices, share), f32),
            pltpu.VMEM((T, slices, bins), bf16),
        ),
        in_specs=[pl.BlockSpec(memory_space=pltpu.HBM)] * 4,
        out_specs=(pl.BlockSpec(memory_space=pltpu.VMEM),) * 2,
        scratch_shapes=[
            pltpu.VMEM((C, KR, bins), bf16),
            pltpu.SMEM(first_tile.shape, jnp.int32),
            pltpu.VMEM((slices + PAD, npix), bf16),
            pltpu.VMEM(system.shape, bf16),
            pltpu.VMEM((T * bins, npix), bf16),
            pltpu.VMEM((T, slices + PAD, bins), f32),
            pltpu.VMEM((slices + PAD, T * bins), bf16),
            [pltpu.VMEM((C, n, bins), bf16) for n in sizes],
            [pltpu.VMEM((G - 1, G * n, share), jnp.int16) for n in sizes],
            [pltpu.VMEM((G - 1, 1, share), f32) for n in sizes],
            pltpu.VMEM((slices, share), f32),
            [pltpu.VMEM((G - 1, G * n, share), jnp.int16) for n in sizes],
            [pltpu.VMEM((G - 1, 1, share), f32) for n in sizes],
            pltpu.VMEM((G, 8, share), f32),
            pltpu.VMEM((G - 1, 8, share), f32),
            dma,
            dma,
            dma((NC, G)),
            dma,
            dma((NC, 2)),
            dma((NC,)),
            pltpu.SemaphoreType.REGULAR((max(NC, 2),)),
            pltpu.SemaphoreType.REGULAR,
            dma((NC, G - 1)),
            dma((NC, G - 1)),
            dma((NC, G - 1)),
            dma((NC, G - 1)),
            dma((G - 1,)),
            dma,
        ],
        compiler_params=pltpu.CompilerParams(
            collective_id=0, has_side_effects=True, vmem_limit_bytes=VMEM_BYTES - out_bytes
        ),
    )(first_tile, projections, start_image, system)
    return pl.pallas_call(
        put_out,
        out_shape=(
            jax.ShapeDtypeStruct(new_image.shape, f32),
            jax.ShapeDtypeStruct(residual.shape, bf16),
        ),
        in_specs=[pl.BlockSpec(memory_space=pl.ANY)] * 2,
        out_specs=(pl.BlockSpec(memory_space=pl.ANY),) * 2,
        scratch_shapes=[dma((2 * PUTS,))],
        compiler_params=pltpu.CompilerParams(vmem_limit_bytes=1 << 20),
    )(new_image, residual)


def solution(mesh):
    in_specs = (
        P("cuts", None, "ang", None, None),
        P("cuts", None),
        P("ang", None, None, None, None),
        P("ang", None),
    )
    out_specs = (P("cuts", "ang"), P("ang", "cuts", None))
    return jax.shard_map(
        functools.partial(on_device, mesh.shape["cuts"], mesh.shape["ang"]),
        mesh=mesh, in_specs=in_specs, out_specs=out_specs, check_vma=False,
    )
```

```python
import functools

import jax
import jax.numpy as jnp
from jax import lax
from jax.experimental import pallas as pl
from jax.experimental.pallas import tpu as pltpu
from jax.sharding import PartitionSpec as P

MESH = pl.DeviceIdType.MESH
NT = (((1,), (1,)), ((), ()))
SPLIT = (2, 2, 2, 2)
TURN = (0, 1, 1, 1)
LATE = 2
PUTS = 2
PAD = 16
STEPS = 32767.0
TINY = 1e-30
ROUND = 12582912.0
VMEM_BYTES = 67043328


def kernel(
    C, G, sizes, first_in, proj, image, system, new_out, res_out,
    held, first, img, sysv, A, F, R, arr, U, unit, own, urecv, unitrecv, colp, crecv,
    held_sem, first_sem, img_sem, sys_sem, send_sem, arr_sem, go_sem, up_sem,
    usend_sem, urecv_sem, nsend_sem, nrecv_sem, csend_sem, crecv_sem,
):
    c = lax.axis_index("cuts")
    a = lax.axis_index("ang")
    T = C // G
    blocks, ptiles, _, W, PW = system.shape
    KR = proj.shape[3]
    NC = len(sizes)
    starts = [sum(sizes[:q]) for q in range(NC)]
    slices, npix = image.shape
    share = npix // G
    bins = proj.shape[4]
    ntiles = bins // W
    pair = PW // W

    tgt = c // T
    slot = a * T + lax.rem(c, T)

    def flip(m):
        o = c
        for b in range(C.bit_length() - 1):
            if (m >> b) & 1:
                o = o + (1 - 2 * lax.rem(c // (1 << b), 2)) * (1 << b)
        return o

    paced = G == 2 and C & (C - 1) == 0 and T > 1
    held_copy = pltpu.make_async_copy(proj.at[0, :, 0], held, held_sem)
    held_copy.start()
    half = T // 2
    inner = tgt + lax.rem(c, T) // max(half, 1) == 1
    outer = jnp.logical_not(inner)
    mate = flip(half) if paced else c
    barrier = pltpu.get_barrier_semaphore()

    def greet(device, where=barrier):
        pl.semaphore_signal(where, inc=1, device_id=device, device_id_type=MESH)

    if paced:
        @pl.when(tgt != a)
        def _():
            for m in range(T, C):
                for s in range(G):
                    greet((flip(m), s))

        for m in range(half):
            for s in range(1 if m == 0 else 0, G):
                greet((flip(m), lax.rem(a + s, G)))

        @pl.when(inner)
        def _():
            greet((mate, a))
    else:
        for i in range(T):
            source = a * T + lax.rem(c + i, T)
            for s in range(1 if i == 0 else 0, G):
                greet((source, lax.rem(a + s, G)))

        @pl.when(tgt != a)
        def _():
            greet((a * T + lax.rem(c, T), a))

        for s in range(1, G):
            greet((c, lax.rem(a + s, G)))

    sys_copy = pltpu.make_async_copy(system, sysv, sys_sem)
    sys_copy.start()
    first_copy = pltpu.make_async_copy(first_in, first, first_sem)
    first_copy.start()
    img_copies = []
    for q in range(NC):
        for b in range(G):
            cp = pltpu.make_async_copy(
                image.at[pl.ds(b * KR + starts[q], sizes[q])],
                img.at[pl.ds(G * starts[q] + b * sizes[q], sizes[q])],
                img_sem.at[q, b],
            )
            cp.start()
            img_copies.append(cp)
    if paced:
        pl.semaphore_wait(barrier, C - T + G * half - 1 + jnp.where(inner, 0, 1))
    else:
        pl.semaphore_wait(barrier, C + G - 2 + jnp.where(tgt == a, 0, 1))

    held_copy.wait()

    def piece(q, o, k=0):
        return pltpu.make_async_remote_copy(
            src_ref=held.at[o, pl.ds(starts[q], sizes[q])],
            dst_ref=arr[q].at[slot],
            send_sem=send_sem.at[q, k],
            recv_sem=arr_sem.at[q],
            device_id=(o, tgt),
            device_id_type=MESH,
        )

    turn = TURN[:NC] if paced and NC == len(TURN) else (0,) * NC
    turns = max(turn) + 1
    AHEAD = 2 if paced else 0
    CROSS = sorted(range(T, C), key=lambda m: (m & half, -(m & (half // 2)), m))

    def send_self(q, k):
        @pl.when(tgt != a)
        def _():
            piece(q, c, k).start()

        @pl.when(tgt == a)
        def _():
            pltpu.make_async_copy(
                held.at[c, pl.ds(starts[q], sizes[q])], arr[q].at[slot], arr_sem.at[q]
            ).start()

    def send_plane(q):
        for m in range(half - 1, 0, -1):
            piece(q, flip(m), 1).start()
        send_self(q, 1)

    def send_half():
        for q in range(NC):
            for m in range(T - 1, half - 1, -1):
                piece(q, flip(m), 1).start()

    def send_ahead(q):
        if AHEAD and q < NC:
            @pl.when(tgt == G - 1)
            def _():
                for o in range(AHEAD):
                    piece(q, o).start()

    def send(q):
        send_ahead(q + 1)
        for m in CROSS:
            o = flip(m)

            @pl.when((tgt != G - 1) | (o >= AHEAD))
            def _(o=o):
                piece(q, o).start()

    def sent_blocks(q, k, n):
        part = held.at[pl.ds(0, n), pl.ds(starts[q], sizes[q])]
        pltpu.make_async_copy(part, part, send_sem.at[q, k]).wait()

    def sent(q):
        sent_blocks(q, 0, C - T)

    def of_turn(k):
        return [q for q in range(NC) if turn[q] == k]

    if paced:
        send_ahead(0)
        for q in of_turn(0):
            send(q)
        if turns > 1:
            @pl.when(inner)
            def _():
                for k in range(1, turns):
                    for q in of_turn(k):
                        send(q)
        for q in range(NC):
            send_plane(q)

        @pl.when(outer)
        def _():
            greet((mate, a), up_sem)
    else:
        for q in range(NC):
            for i in range(1, C):
                piece(q, lax.rem(c + i, C)).start()
            send_self(q, 0)

    def meet():
        pl.semaphore_wait(up_sem, 1)

        @pl.when(inner)
        def _():
            greet((mate, a), up_sem)

        send_half()

    def take_turn(k):
        if k >= turns:
            return

        @pl.when(inner)
        def _():
            for q in of_turn(k - 1):
                sent(q)
            pl.semaphore_signal(go_sem.at[k - 1], inc=1, device_id=(mate, a), device_id_type=MESH)

        @pl.when(outer)
        def _():
            pl.semaphore_wait(go_sem.at[k - 1], 1)
            for q in of_turn(k):
                send(q)

    img[pl.ds(slices, PAD)] = jnp.ones((PAD, npix), jnp.bfloat16)
    R[pl.ds(0, PAD)] = jnp.ones((PAD, T * bins), jnp.bfloat16)
    sys_copy.wait()
    first_copy.wait()

    def build(i, carry):
        lane = lax.broadcasted_iota(jnp.int32, (W, pair * W), 1) // W
        cols = pl.ds(pl.multiple_of(i * pair * W, pair * W), pair * W)
        for g in range(blocks):
            x = [
                jnp.concatenate([sysv[g, i * pair + k, j] for k in range(pair)], axis=0)
                .astype(jnp.float32).T.astype(jnp.bfloat16)
                for j in range(2)
            ]
            f = jnp.full(lane.shape, first[g, i * pair], jnp.int32)
            for k in range(1, pair):
                f = jnp.where(lane == k, first[g, i * pair + k], f)
            second = jnp.where(f == ntiles - 1, 0, f + 1)
            for b in range(ntiles):
                m0, m1 = f == b, second == b
                for t in range(pair):
                    part = slice(t * W, (t + 1) * W)
                    tile = jnp.where(m0, x[0][part], jnp.where(m1, x[1][part], jnp.zeros((), jnp.bfloat16)))
                    A[pl.ds((g * pair + t) * bins + b * W, W), cols] = tile
        return carry

    lax.fori_loop(0, ptiles // pair, build, 0)
    if paced:
        meet()

    for cp in img_copies:
        cp.wait()

    def project(t, carry):
        m = A[pl.ds(pl.multiple_of(t * bins, bins), bins)]
        F[t] = lax.dot_general(img[...], m, NT, preferred_element_type=jnp.float32)
        return carry

    lax.fori_loop(0, T, project, 0)

    def residual_part(q):
        def body(t, carry):
            scale = 1.0 / F[t, pl.ds(slices, 8)][:1]
            for b in range(G):
                value = arr[q][b * T + t].astype(jnp.float32)
                f = F[t, pl.ds(G * starts[q] + b * sizes[q], sizes[q])]
                res = ((value - f) * scale).astype(jnp.bfloat16)
                R[
                    pl.ds(PAD + G * starts[q] + b * sizes[q], sizes[q]),
                    pl.ds(pl.multiple_of(t * bins, bins), bins),
                ] = res
                res_out[t, pl.ds(b * KR + starts[q], sizes[q])] = res
            return carry

        lax.fori_loop(0, T, body, 0)

    def back(lo, hi, g):
        return jnp.dot(
            R[pl.ds(lo, hi - lo)],
            A[:, pl.ds(pl.multiple_of(g * share, share), share)],
            preferred_element_type=jnp.float32,
        )

    def col_copy(s):
        g = lax.rem(a + s, G)
        return pltpu.make_async_remote_copy(
            src_ref=colp.at[g], dst_ref=crecv.at[s - 1], send_sem=csend_sem.at[s - 1],
            recv_sem=crecv_sem, device_id=(c, g), device_id_type=MESH,
        )

    def u_copy(q, s):
        g = lax.rem(a + s, G)
        return pltpu.make_async_remote_copy(
            src_ref=U[q].at[s - 1], dst_ref=urecv[q].at[s - 1],
            send_sem=usend_sem.at[q, s - 1], recv_sem=urecv_sem.at[q, s - 1],
            device_id=(c, g), device_id_type=MESH,
        )

    def unit_copy(q, s):
        g = lax.rem(a + s, G)
        return pltpu.make_async_remote_copy(
            src_ref=unit[q].at[s - 1], dst_ref=unitrecv[q].at[s - 1],
            send_sem=nsend_sem.at[q, s - 1], recv_sem=nrecv_sem.at[q, s - 1],
            device_id=(c, g), device_id_type=MESH,
        )

    def own_back(lo, hi):
        y = back(lo, hi, a)
        if lo == 0:
            colp[a] = y[:8]
            y = y[PAD:]
            lo = PAD
        own[pl.ds(lo - PAD, hi - lo)] = y

    def process(q):
        pltpu.make_async_copy(arr[q], arr[q], arr_sem.at[q]).wait()
        residual_part(q)
        lo = 0 if q == 0 else PAD + G * starts[q]
        hi = PAD + G * (starts[q] + sizes[q])
        for s in range(1, G):
            y = back(lo, hi, lax.rem(a + s, G))
            if q == 0:
                colp[lax.rem(a + s, G)] = y[:8]
                y = y[PAD:]
            top = jnp.maximum(jnp.max(jnp.abs(y), axis=0, keepdims=True), TINY)
            unit[q][s - 1] = top * (1.0 / STEPS)
            U[q][s - 1] = ((y * (STEPS / top) + ROUND) - ROUND).astype(jnp.int32).astype(jnp.int16)
            unit_copy(q, s).start()
            u_copy(q, s).start()
            if q == 0:
                col_copy(s).start()
        late = max(NC - LATE, 0)
        if q < late:
            own_back(lo, hi)
        elif q == NC - 1:
            own_back(0 if late == 0 else PAD + G * starts[late], hi)

    def prepare(own_inv):
        mine = img[pl.ds(0, slices), pl.ds(pl.multiple_of(a * share, share), share)]
        own[...] = mine.astype(jnp.float32) + own[...] * own_inv

    def finish(q, own_inv):
        new = own[pl.ds(G * starts[q], G * sizes[q])]
        for s in range(1, G):
            unit_copy(q, s).wait_recv()
            scale = unitrecv[q][s - 1] * own_inv
            u_copy(q, s).wait_recv()
            new = new + urecv[q][s - 1].astype(jnp.int32).astype(jnp.float32) * scale
        for b in range(G):
            new_out[pl.ds(b * KR + starts[q], sizes[q])] = new[b * sizes[q] : (b + 1) * sizes[q]]

    take_turn(1)
    for q in range(NC):
        process(q)
        take_turn(q + 2)

    pltpu.make_async_copy(crecv, crecv, crecv_sem).wait()
    columns = colp[a][:1]
    for s in range(1, G):
        columns = columns + crecv[s - 1][:1]
    own_inv = 1.0 / columns
    prepare(own_inv)
    for q in range(NC - 1):
        finish(q, own_inv)

    for q in range(NC):
        if not paced:
            @pl.when(tgt == a)
            def _(q=q):
                sent_blocks(q, 0, C - 1)

            @pl.when(tgt != a)
            def _(q=q):
                sent_blocks(q, 0, C)

            continue
        if turn[q] == turns - 1:
            sent(q)
        else:
            @pl.when(outer)
            def _(q=q):
                sent(q)

        @pl.when(tgt == a)
        def _(q=q):
            sent_blocks(q, 1, T - 1)

        @pl.when(tgt != a)
        def _(q=q):
            sent_blocks(q, 1, T)

    for s in range(1, G):
        col_copy(s).wait_send()
    for q in range(NC):
        if q == NC - 1:
            finish(q, own_inv)
        for s in range(1, G):
            u_copy(q, s).wait_send()
            unit_copy(q, s).wait_send()


def put_out(new_in, res_in, new_out, res_out, sem):
    copies = []
    for i, (src, dst) in enumerate(((new_in, new_out), (res_in, res_out))):
        n = src.shape[0] // PUTS
        for k in range(PUTS):
            part = pl.ds(k * n, n)
            copies.append(pltpu.make_async_copy(src.at[part], dst.at[part], sem.at[i * PUTS + k]))
    for cp in copies:
        cp.start()
    for cp in copies:
        cp.wait()


def chunk_sizes(rows):
    unit = max(16, rows // sum(SPLIT))
    sizes = [n * unit for n in SPLIT]
    if sum(sizes) == rows:
        return sizes
    return [16] * (rows // 16) if rows % 16 == 0 else [rows]


def on_device(C, G, projections, start_image, system, first_tile):
    T = C // G
    KR = projections.shape[3]
    sizes = chunk_sizes(KR)
    NC = len(sizes)
    slices, npix = start_image.shape
    bins = projections.shape[4]
    share = npix // G
    bf16, f32 = jnp.bfloat16, jnp.float32
    dma = pltpu.SemaphoreType.DMA
    out_bytes = slices * share * 4 + T * slices * bins * 2
    new_image, residual = pl.pallas_call(
        functools.partial(kernel, C, G, sizes),
        out_shape=(
            pltpu.VMEM((slices, share), f32),
            pltpu.VMEM((T, slices, bins), bf16),
        ),
        in_specs=[pl.BlockSpec(memory_space=pltpu.HBM)] * 4,
        out_specs=(pl.BlockSpec(memory_space=pltpu.VMEM),) * 2,
        scratch_shapes=[
            pltpu.VMEM((C, KR, bins), bf16),
            pltpu.SMEM(first_tile.shape, jnp.int32),
            pltpu.VMEM((slices + PAD, npix), bf16),
            pltpu.VMEM(system.shape, bf16),
            pltpu.VMEM((T * bins, npix), bf16),
            pltpu.VMEM((T, slices + PAD, bins), f32),
            pltpu.VMEM((slices + PAD, T * bins), bf16),
            [pltpu.VMEM((C, n, bins), bf16) for n in sizes],
            [pltpu.VMEM((G - 1, G * n, share), jnp.int16) for n in sizes],
            [pltpu.VMEM((G - 1, 1, share), f32) for n in sizes],
            pltpu.VMEM((slices, share), f32),
            [pltpu.VMEM((G - 1, G * n, share), jnp.int16) for n in sizes],
            [pltpu.VMEM((G - 1, 1, share), f32) for n in sizes],
            pltpu.VMEM((G, 8, share), f32),
            pltpu.VMEM((G - 1, 8, share), f32),
            dma,
            dma,
            dma((NC, G)),
            dma,
            dma((NC, 2)),
            dma((NC,)),
            pltpu.SemaphoreType.REGULAR((max(NC, 2),)),
            pltpu.SemaphoreType.REGULAR,
            dma((NC, G - 1)),
            dma((NC, G - 1)),
            dma((NC, G - 1)),
            dma((NC, G - 1)),
            dma((G - 1,)),
            dma,
        ],
        compiler_params=pltpu.CompilerParams(
            collective_id=0, has_side_effects=True, vmem_limit_bytes=VMEM_BYTES - out_bytes
        ),
    )(first_tile, projections, start_image, system)
    return pl.pallas_call(
        put_out,
        out_shape=(
            jax.ShapeDtypeStruct(new_image.shape, f32),
            jax.ShapeDtypeStruct(residual.shape, bf16),
        ),
        in_specs=[pl.BlockSpec(memory_space=pl.ANY)] * 2,
        out_specs=(pl.BlockSpec(memory_space=pl.ANY),) * 2,
        scratch_shapes=[dma((2 * PUTS,))],
        compiler_params=pltpu.CompilerParams(vmem_limit_bytes=1 << 20),
    )(new_image, residual)


def solution(mesh):
    in_specs = (
        P("cuts", None, "ang", None, None),
        P("cuts", None),
        P("ang", None, None, None, None),
        P("ang", None),
    )
    out_specs = (P("cuts", "ang"), P("ang", "cuts", None))
    return jax.shard_map(
        functools.partial(on_device, mesh.shape["cuts"], mesh.shape["ang"]),
        mesh=mesh, in_specs=in_specs, out_specs=out_specs, check_vma=False,
    )
```

```python
import functools

import jax
import jax.numpy as jnp
from jax import lax
from jax.experimental import pallas as pl
from jax.experimental.pallas import tpu as pltpu
from jax.sharding import PartitionSpec as P

MESH = pl.DeviceIdType.MESH
NT = (((1,), (1,)), ((), ()))
SPLIT = (2, 2, 2, 2)
TURN = (0, 1, 2, 2)
LATE = 2
PUTS = 1
PAD = 16
STEPS = 32767.0
TINY = 1e-30
ROUND = 12582912.0
VMEM_BYTES = 67043328


def kernel(
    C, G, sizes, first_in, proj, image, system, new_out, res_out,
    held, first, img, sysv, A, F, R, arr, U, unit, own, urecv, unitrecv, colp, crecv,
    held_sem, first_sem, img_sem, sys_sem, send_sem, arr_sem, go_sem, up_sem,
    usend_sem, urecv_sem, nsend_sem, nrecv_sem, csend_sem, crecv_sem,
):
    c = lax.axis_index("cuts")
    a = lax.axis_index("ang")
    T = C // G
    blocks, ptiles, _, W, PW = system.shape
    KR = proj.shape[3]
    NC = len(sizes)
    starts = [sum(sizes[:q]) for q in range(NC)]
    slices, npix = image.shape
    share = npix // G
    bins = proj.shape[4]
    ntiles = bins // W
    pair = PW // W

    tgt = c // T
    slot = a * T + lax.rem(c, T)

    def flip(m):
        o = c
        for b in range(C.bit_length() - 1):
            if (m >> b) & 1:
                o = o + (1 - 2 * lax.rem(c // (1 << b), 2)) * (1 << b)
        return o

    paced = G == 2 and C & (C - 1) == 0 and T > 1
    held_copy = pltpu.make_async_copy(proj.at[0, :, 0], held, held_sem)
    held_copy.start()
    half = T // 2
    inner = tgt + lax.rem(c, T) // max(half, 1) == 1
    outer = jnp.logical_not(inner)
    mate = flip(half) if paced else c
    barrier = pltpu.get_barrier_semaphore()

    def greet(device, where=barrier):
        pl.semaphore_signal(where, inc=1, device_id=device, device_id_type=MESH)

    if paced:
        @pl.when(tgt != a)
        def _():
            for m in range(T, C):
                for s in range(G):
                    greet((flip(m), s))

        for m in range(half):
            for s in range(1 if m == 0 else 0, G):
                greet((flip(m), lax.rem(a + s, G)))

        @pl.when(inner)
        def _():
            greet((mate, a))
    else:
        for i in range(T):
            source = a * T + lax.rem(c + i, T)
            for s in range(1 if i == 0 else 0, G):
                greet((source, lax.rem(a + s, G)))

        @pl.when(tgt != a)
        def _():
            greet((a * T + lax.rem(c, T), a))

        for s in range(1, G):
            greet((c, lax.rem(a + s, G)))

    sys_copy = pltpu.make_async_copy(system, sysv, sys_sem)
    sys_copy.start()
    first_copy = pltpu.make_async_copy(first_in, first, first_sem)
    first_copy.start()
    img_copies = []
    for q in range(NC):
        for b in range(G):
            cp = pltpu.make_async_copy(
                image.at[pl.ds(b * KR + starts[q], sizes[q])],
                img.at[pl.ds(G * starts[q] + b * sizes[q], sizes[q])],
                img_sem.at[q, b],
            )
            cp.start()
            img_copies.append(cp)
    if paced:
        pl.semaphore_wait(barrier, C - T + G * half - 1 + jnp.where(inner, 0, 1))
    else:
        pl.semaphore_wait(barrier, C + G - 2 + jnp.where(tgt == a, 0, 1))

    held_copy.wait()

    def piece(q, o, k=0):
        return pltpu.make_async_remote_copy(
            src_ref=held.at[o, pl.ds(starts[q], sizes[q])],
            dst_ref=arr[q].at[slot],
            send_sem=send_sem.at[q, k],
            recv_sem=arr_sem.at[q],
            device_id=(o, tgt),
            device_id_type=MESH,
        )

    turn = TURN[:NC] if paced and NC == len(TURN) else (0,) * NC
    turns = max(turn) + 1
    AHEAD = 2 if paced else 0
    CROSS = sorted(range(T, C), key=lambda m: (m & half, -(m & (half // 2)), m))

    def send_self(q, k):
        @pl.when(tgt != a)
        def _():
            piece(q, c, k).start()

        @pl.when(tgt == a)
        def _():
            pltpu.make_async_copy(
                held.at[c, pl.ds(starts[q], sizes[q])], arr[q].at[slot], arr_sem.at[q]
            ).start()

    def send_plane(q):
        for m in range(half - 1, 0, -1):
            piece(q, flip(m), 1).start()
        send_self(q, 1)

    def send_half():
        for q in range(NC):
            for m in range(T - 1, half - 1, -1):
                piece(q, flip(m), 1).start()

    def send_ahead(q):
        if AHEAD and q < NC:
            @pl.when(tgt == G - 1)
            def _():
                for o in range(AHEAD):
                    piece(q, o).start()

    def send(q):
        send_ahead(q + 1)
        for m in CROSS:
            o = flip(m)

            @pl.when((tgt != G - 1) | (o >= AHEAD))
            def _(o=o):
                piece(q, o).start()

    def sent_blocks(q, k, n):
        part = held.at[pl.ds(0, n), pl.ds(starts[q], sizes[q])]
        pltpu.make_async_copy(part, part, send_sem.at[q, k]).wait()

    def sent(q):
        sent_blocks(q, 0, C - T)

    def of_turn(k):
        return [q for q in range(NC) if turn[q] == k]

    if paced:
        send_ahead(0)
        for q in of_turn(0):
            send(q)
        if turns > 1:
            @pl.when(inner)
            def _():
                for k in range(1, turns):
                    for q in of_turn(k):
                        send(q)
        for q in range(NC):
            send_plane(q)

        @pl.when(outer)
        def _():
            greet((mate, a), up_sem)
    else:
        for q in range(NC):
            for i in range(1, C):
                piece(q, lax.rem(c + i, C)).start()
            send_self(q, 0)

    def meet():
        pl.semaphore_wait(up_sem, 1)

        @pl.when(inner)
        def _():
            greet((mate, a), up_sem)

        send_half()

    def take_turn(k):
        if k >= turns:
            return

        @pl.when(inner)
        def _():
            for q in of_turn(k - 1):
                sent(q)
            pl.semaphore_signal(go_sem.at[k - 1], inc=1, device_id=(mate, a), device_id_type=MESH)

        @pl.when(outer)
        def _():
            pl.semaphore_wait(go_sem.at[k - 1], 1)
            for q in of_turn(k):
                send(q)

    img[pl.ds(slices, PAD)] = jnp.ones((PAD, npix), jnp.bfloat16)
    R[pl.ds(0, PAD)] = jnp.ones((PAD, T * bins), jnp.bfloat16)
    sys_copy.wait()
    first_copy.wait()

    def build(i, carry):
        lane = lax.broadcasted_iota(jnp.int32, (W, pair * W), 1) // W
        cols = pl.ds(pl.multiple_of(i * pair * W, pair * W), pair * W)
        for g in range(blocks):
            x = [
                jnp.concatenate([sysv[g, i * pair + k, j] for k in range(pair)], axis=0)
                .astype(jnp.float32).T.astype(jnp.bfloat16)
                for j in range(2)
            ]
            f = jnp.full(lane.shape, first[g, i * pair], jnp.int32)
            for k in range(1, pair):
                f = jnp.where(lane == k, first[g, i * pair + k], f)
            second = jnp.where(f == ntiles - 1, 0, f + 1)
            for b in range(ntiles):
                m0, m1 = f == b, second == b
                for t in range(pair):
                    part = slice(t * W, (t + 1) * W)
                    tile = jnp.where(m0, x[0][part], jnp.where(m1, x[1][part], jnp.zeros((), jnp.bfloat16)))
                    A[pl.ds((g * pair + t) * bins + b * W, W), cols] = tile
        return carry

    lax.fori_loop(0, ptiles // pair, build, 0)
    if paced:
        meet()

    for cp in img_copies:
        cp.wait()

    def project(t, carry):
        m = A[pl.ds(pl.multiple_of(t * bins, bins), bins)]
        F[t] = lax.dot_general(img[...], m, NT, preferred_element_type=jnp.float32)
        return carry

    lax.fori_loop(0, T, project, 0)

    def residual_part(q):
        def body(t, carry):
            scale = 1.0 / F[t, pl.ds(slices, 8)][:1]
            for b in range(G):
                value = arr[q][b * T + t].astype(jnp.float32)
                f = F[t, pl.ds(G * starts[q] + b * sizes[q], sizes[q])]
                res = ((value - f) * scale).astype(jnp.bfloat16)
                R[
                    pl.ds(PAD + G * starts[q] + b * sizes[q], sizes[q]),
                    pl.ds(pl.multiple_of(t * bins, bins), bins),
                ] = res
                res_out[t, pl.ds(b * KR + starts[q], sizes[q])] = res
            return carry

        lax.fori_loop(0, T, body, 0)

    def back(lo, hi, g):
        return jnp.dot(
            R[pl.ds(lo, hi - lo)],
            A[:, pl.ds(pl.multiple_of(g * share, share), share)],
            preferred_element_type=jnp.float32,
        )

    def col_copy(s):
        g = lax.rem(a + s, G)
        return pltpu.make_async_remote_copy(
            src_ref=colp.at[g], dst_ref=crecv.at[s - 1], send_sem=csend_sem.at[s - 1],
            recv_sem=crecv_sem, device_id=(c, g), device_id_type=MESH,
        )

    def u_copy(q, s):
        g = lax.rem(a + s, G)
        return pltpu.make_async_remote_copy(
            src_ref=U[q].at[s - 1], dst_ref=urecv[q].at[s - 1],
            send_sem=usend_sem.at[q, s - 1], recv_sem=urecv_sem.at[q, s - 1],
            device_id=(c, g), device_id_type=MESH,
        )

    def unit_copy(q, s):
        g = lax.rem(a + s, G)
        return pltpu.make_async_remote_copy(
            src_ref=unit[q].at[s - 1], dst_ref=unitrecv[q].at[s - 1],
            send_sem=nsend_sem.at[q, s - 1], recv_sem=nrecv_sem.at[q, s - 1],
            device_id=(c, g), device_id_type=MESH,
        )

    def own_back(lo, hi):
        y = back(lo, hi, a)
        if lo == 0:
            colp[a] = y[:8]
            y = y[PAD:]
            lo = PAD
        own[pl.ds(lo - PAD, hi - lo)] = y

    def process(q):
        pltpu.make_async_copy(arr[q], arr[q], arr_sem.at[q]).wait()
        residual_part(q)
        lo = 0 if q == 0 else PAD + G * starts[q]
        hi = PAD + G * (starts[q] + sizes[q])
        for s in range(1, G):
            y = back(lo, hi, lax.rem(a + s, G))
            if q == 0:
                colp[lax.rem(a + s, G)] = y[:8]
                y = y[PAD:]
            top = jnp.maximum(jnp.max(jnp.abs(y), axis=0, keepdims=True), TINY)
            unit[q][s - 1] = top * (1.0 / STEPS)
            U[q][s - 1] = ((y * (STEPS / top) + ROUND) - ROUND).astype(jnp.int32).astype(jnp.int16)
            unit_copy(q, s).start()
            u_copy(q, s).start()
            if q == 0:
                col_copy(s).start()
        late = max(NC - LATE, 0)
        if q < late:
            own_back(lo, hi)
        elif q == NC - 1:
            own_back(0 if late == 0 else PAD + G * starts[late], hi)

    def prepare(own_inv):
        mine = img[pl.ds(0, slices), pl.ds(pl.multiple_of(a * share, share), share)]
        own[...] = mine.astype(jnp.float32) + own[...] * own_inv

    def finish(q, own_inv):
        new = own[pl.ds(G * starts[q], G * sizes[q])]
        for s in range(1, G):
            unit_copy(q, s).wait_recv()
            scale = unitrecv[q][s - 1] * own_inv
            u_copy(q, s).wait_recv()
            new = new + urecv[q][s - 1].astype(jnp.int32).astype(jnp.float32) * scale
        for b in range(G):
            new_out[pl.ds(b * KR + starts[q], sizes[q])] = new[b * sizes[q] : (b + 1) * sizes[q]]

    take_turn(1)
    for q in range(NC):
        process(q)
        take_turn(q + 2)

    pltpu.make_async_copy(crecv, crecv, crecv_sem).wait()
    columns = colp[a][:1]
    for s in range(1, G):
        columns = columns + crecv[s - 1][:1]
    own_inv = 1.0 / columns
    prepare(own_inv)
    for q in range(NC - 1):
        finish(q, own_inv)

    for q in range(NC):
        if not paced:
            @pl.when(tgt == a)
            def _(q=q):
                sent_blocks(q, 0, C - 1)

            @pl.when(tgt != a)
            def _(q=q):
                sent_blocks(q, 0, C)

            continue
        if turn[q] == turns - 1:
            sent(q)
        else:
            @pl.when(outer)
            def _(q=q):
                sent(q)

        @pl.when(tgt == a)
        def _(q=q):
            sent_blocks(q, 1, T - 1)

        @pl.when(tgt != a)
        def _(q=q):
            sent_blocks(q, 1, T)

    for s in range(1, G):
        col_copy(s).wait_send()
    for q in range(NC):
        if q == NC - 1:
            finish(q, own_inv)
        for s in range(1, G):
            u_copy(q, s).wait_send()
            unit_copy(q, s).wait_send()


def put_out(new_in, res_in, new_out, res_out, sem):
    copies = []
    for i, (src, dst) in enumerate(((new_in, new_out), (res_in, res_out))):
        n = src.shape[0] // PUTS
        for k in range(PUTS):
            part = pl.ds(k * n, n)
            copies.append(pltpu.make_async_copy(src.at[part], dst.at[part], sem.at[i * PUTS + k]))
    for cp in copies:
        cp.start()
    for cp in copies:
        cp.wait()


def chunk_sizes(rows):
    unit = max(16, rows // sum(SPLIT))
    sizes = [n * unit for n in SPLIT]
    if sum(sizes) == rows:
        return sizes
    return [16] * (rows // 16) if rows % 16 == 0 else [rows]


def on_device(C, G, projections, start_image, system, first_tile):
    T = C // G
    KR = projections.shape[3]
    sizes = chunk_sizes(KR)
    NC = len(sizes)
    slices, npix = start_image.shape
    bins = projections.shape[4]
    share = npix // G
    bf16, f32 = jnp.bfloat16, jnp.float32
    dma = pltpu.SemaphoreType.DMA
    out_bytes = slices * share * 4 + T * slices * bins * 2
    new_image, residual = pl.pallas_call(
        functools.partial(kernel, C, G, sizes),
        out_shape=(
            pltpu.VMEM((slices, share), f32),
            pltpu.VMEM((T, slices, bins), bf16),
        ),
        in_specs=[pl.BlockSpec(memory_space=pltpu.HBM)] * 4,
        out_specs=(pl.BlockSpec(memory_space=pltpu.VMEM),) * 2,
        scratch_shapes=[
            pltpu.VMEM((C, KR, bins), bf16),
            pltpu.SMEM(first_tile.shape, jnp.int32),
            pltpu.VMEM((slices + PAD, npix), bf16),
            pltpu.VMEM(system.shape, bf16),
            pltpu.VMEM((T * bins, npix), bf16),
            pltpu.VMEM((T, slices + PAD, bins), f32),
            pltpu.VMEM((slices + PAD, T * bins), bf16),
            [pltpu.VMEM((C, n, bins), bf16) for n in sizes],
            [pltpu.VMEM((G - 1, G * n, share), jnp.int16) for n in sizes],
            [pltpu.VMEM((G - 1, 1, share), f32) for n in sizes],
            pltpu.VMEM((slices, share), f32),
            [pltpu.VMEM((G - 1, G * n, share), jnp.int16) for n in sizes],
            [pltpu.VMEM((G - 1, 1, share), f32) for n in sizes],
            pltpu.VMEM((G, 8, share), f32),
            pltpu.VMEM((G - 1, 8, share), f32),
            dma,
            dma,
            dma((NC, G)),
            dma,
            dma((NC, 2)),
            dma((NC,)),
            pltpu.SemaphoreType.REGULAR((max(NC, 2),)),
            pltpu.SemaphoreType.REGULAR,
            dma((NC, G - 1)),
            dma((NC, G - 1)),
            dma((NC, G - 1)),
            dma((NC, G - 1)),
            dma((G - 1,)),
            dma,
        ],
        compiler_params=pltpu.CompilerParams(
            collective_id=0, has_side_effects=True, vmem_limit_bytes=VMEM_BYTES - out_bytes
        ),
    )(first_tile, projections, start_image, system)
    return pl.pallas_call(
        put_out,
        out_shape=(
            jax.ShapeDtypeStruct(new_image.shape, f32),
            jax.ShapeDtypeStruct(residual.shape, bf16),
        ),
        in_specs=[pl.BlockSpec(memory_space=pl.ANY)] * 2,
        out_specs=(pl.BlockSpec(memory_space=pl.ANY),) * 2,
        scratch_shapes=[dma((2 * PUTS,))],
        compiler_params=pltpu.CompilerParams(vmem_limit_bytes=1 << 20),
    )(new_image, residual)


def solution(mesh):
    in_specs = (
        P("cuts", None, "ang", None, None),
        P("cuts", None),
        P("ang", None, None, None, None),
        P("ang", None),
    )
    out_specs = (P("cuts", "ang"), P("ang", "cuts", None))
    return jax.shard_map(
        functools.partial(on_device, mesh.shape["cuts"], mesh.shape["ang"]),
        mesh=mesh, in_specs=in_specs, out_specs=out_specs, check_vma=False,
    )
```
